512 devices in a mesh: dp: 4 (over x), context: 16 (over z, core), tensor: 8 (over y).
Axes of the slice: x: 4, y: 8, z: 8, core: 2. Of those that a mesh axis runs over, the one named last changes fastest.
Arguments:
- queries: bfloat16 [16384, 8192], P(('dp', 'context', 'tensor')), may hold values from -5 to 5
- keys: bfloat16 [16384, 1024], P(('dp', 'context', 'tensor')), may hold values from -5 to 5
- values: bfloat16 [16384, 1024], P(('dp', 'context', 'tensor')), may hold values from -6 to 6
- grad_out: bfloat16 [16384, 8192], P(('dp', 'context', 'tensor')), may hold values from -6 to 6
- doc_lengths: int32 [4, 32], replicated, may hold values from 1 to 512, 4096 in all within a row
- deal_plan: int32 [16, 4, 8, 4], replicated, may hold values from 0 to 3, each once within a row
Outputs:
- attention_output: bfloat16 [16384, 8192], P(('dp', 'context'), 'tensor')
- query_gradient: bfloat16 [16384, 8192], P(('dp', 'context'), 'tensor')
- key_gradient: bfloat16 [16384, 1024], P(('dp', 'context'), 'tensor')
- value_gradient: bfloat16 [16384, 1024], P(('dp', 'context'), 'tensor')
The draws below stay inside these ranges and needn't reach their ends.
Inputs may be any that keep to these rules, and one draw needn't show every extreme that they name: Each row of doc_lengths sums to 4096 and its largest entry is exactly 512. `deal_plan`: each row along the last dimension names every replica once.
All inputs are finite; a program needn't handle non-finite values.
Results may differ from the reference program's by a relative error of at most 0.012.
The reference program's roundings to bfloat16 on the way (of `probs_b` and `dscore`) count: a program that leaves them out, or rounds other values in their place, can miss the bound.
Values may be sent and summed in bfloat16 or wider, within the bound.
A program may use at most 64 MiB of HBM per device.

```python
import math
import jax
import jax.numpy as jnp
import numpy as np
from jax import lax

QUERY_HEADS = 64
KEY_VALUE_HEADS = 8
HEAD_SIZE = 128
TOK_DEV = 256
MOST = 512
QUERY_GROUP = 8
SEQUENCE_LENGTH = 4096
TOTAL_ROWS = 16384
NDOCS = 32
REACH = 2
N_DP = 4
N_CONTEXT = 16
N_TENSOR = 8


def draw_pair(key):
    every_row = N_DP * N_CONTEXT * TOK_DEV
    key_query = jax.random.fold_in(key, 101)
    random_key_seed = jax.random.fold_in(key, 202)
    queries = jnp.clip(jax.random.normal(key_query, (every_row, QUERY_HEADS * HEAD_SIZE), jnp.float32), -5.0, 5.0)
    keys = jnp.clip(jax.random.normal(random_key_seed, (every_row, KEY_VALUE_HEADS * HEAD_SIZE), jnp.float32), -5.0, 5.0)
    return (queries, keys)


def draw_queries(key, part):
    return draw_pair(key)[0].astype(jnp.bfloat16)


def draw_keys(key, part):
    return draw_pair(key)[1].astype(jnp.bfloat16)


def shard_levels(own_key, dims, cuts, least, high):
    gain, own = 1.0, jax.random.fold_in(own_key, 6)
    for axis_at, blocks in cuts:
        steps = jnp.exp(jax.random.uniform(jax.random.fold_in(own, axis_at), (blocks,), jnp.float32, least / len(cuts), high / len(cuts)))
        gain = gain * jnp.repeat(steps, dims[axis_at] // blocks).reshape([-1 if axis == axis_at else 1 for axis in range(len(dims))])
    return gain


def split_up(count, total, reach, lean):
    weights = [(1 << 20) // math.isqrt(standing ** lean) + 1 for standing in range(2, count + 1)]
    surplus, given = total - reach - (count - 1), [1] * (count - 1)
    while surplus > 0:
        candidates = [i for i in range(count - 1) if given[i] < reach]
        whole, budget = sum([weights[i] for i in candidates]), surplus
        for i in candidates:
            more = min(reach - given[i], max(1, budget * weights[i] // whole), surplus)
            given[i] = given[i] + more
            surplus = surplus - more
    return np.array([reach] + given)


def ragged_sizes(rng, amount, total, limit, slope):
    if amount == 2:
        one = jax.random.randint(rng, (), max(1, total - limit), min(limit, total - 1) + 1)
        return jnp.stack([one, total - one])
    lengths = jnp.asarray(split_up(amount, total, limit, slope), jnp.int32)
    couples = (amount - 1) // 2
    giver, receiver = lengths[1:1 + 2 * couples:2], lengths[2:2 + 2 * couples:2]
    margin = jnp.minimum(giver - 1, limit - receiver)
    moved = jax.random.randint(jax.random.fold_in(rng, 1), (couples,), 0, 1 << 20) % (margin + 1)
    lengths = lengths.at[1:1 + 2 * couples:2].set(giver - moved).at[2:2 + 2 * couples:2].set(receiver + moved)
    return lengths[jax.random.permutation(jax.random.fold_in(rng, 2), amount)]


def gaussian(key, extent, spread, most, pieces=(), kind=jnp.bfloat16):
    array = spread * jax.random.normal(key, extent, jnp.float32)
    if pieces:
        array = array * shard_levels(key, extent, pieces, -0.22, 0.18)
    return jnp.clip(array, -most, most).astype(kind)


def setup_inputs(seed: int = 0) -> dict:
    key_list = jax.random.split(jax.random.key(seed), 7)
    queries = draw_queries(jax.random.fold_in(key_list[6], 71), 0)
    keys = draw_keys(jax.random.fold_in(key_list[6], 71), 0)
    values = gaussian(key_list[2], (TOTAL_ROWS, KEY_VALUE_HEADS * HEAD_SIZE), 1.0, 6.0, ((0, 512),))
    grad_out = gaussian(key_list[3], (TOTAL_ROWS, QUERY_HEADS * HEAD_SIZE), 1.0, 6.0, ((0, 512),))
    doc_lengths = jax.vmap(lambda own: ragged_sizes(own, NDOCS, SEQUENCE_LENGTH, MOST, 2))(jax.random.split(key_list[4], N_DP)).reshape((N_DP, NDOCS)).astype(jnp.int32)
    deal_plan = jax.vmap(lambda own: jax.random.permutation(own, N_DP))(jax.random.split(key_list[5], N_CONTEXT * N_DP * N_TENSOR)).reshape((N_CONTEXT, N_DP, N_TENSOR, N_DP)).astype(jnp.int32)
    return {"queries": queries, "keys": keys, "values": values, "grad_out": grad_out, "doc_lengths": doc_lengths, "deal_plan": deal_plan}


masked_score = -1.0e30


def deal_rows(matrix, deal_plan):
    width_all = matrix.shape[1]
    sub_rows = TOK_DEV // (N_DP * N_TENSOR)
    source = matrix.reshape(N_DP, N_CONTEXT, N_TENSOR, N_DP, sub_rows, width_all)
    replica_ids = jnp.arange(N_DP, dtype=jnp.int32)
    chosen = jnp.sum(replica_ids * (deal_plan[:, :, :, None, :] == replica_ids[:, None]).astype(jnp.int32), axis=-1)
    chosen = chosen.transpose(1, 0, 2, 3)
    src_ids = jnp.arange(N_DP, dtype=jnp.int32)[:, None, None, None]
    ctx_ids = jnp.arange(N_CONTEXT, dtype=jnp.int32)[None, :, None, None]
    lane_ids = jnp.arange(N_TENSOR, dtype=jnp.int32)[None, None, :, None]
    picked = source[src_ids, ctx_ids, lane_ids, chosen]
    return picked.transpose(3, 1, 0, 2, 4, 5).reshape(N_DP * N_CONTEXT * TOK_DEV, width_all)


def attend(query_sequence, key_sequence, value_sequence, output_gradient_sequence, seg_ids):
    reach_rows = REACH * TOK_DEV
    window = (REACH + 1) * TOK_DEV
    k_pad = jnp.concatenate([jnp.zeros((reach_rows, HEAD_SIZE), key_sequence.dtype), key_sequence], axis=0)
    v_pad = jnp.concatenate([jnp.zeros((reach_rows, HEAD_SIZE), value_sequence.dtype), value_sequence], axis=0)
    seg_pad = jnp.concatenate([jnp.full((reach_rows,), -1, jnp.int32), seg_ids.astype(jnp.int32)])
    pos_pad = jnp.arange(SEQUENCE_LENGTH + reach_rows, dtype=jnp.int32) - reach_rows
    score_scale = HEAD_SIZE ** -0.5

    def block(carry, index):
        dk_pad, dv_pad = carry
        start = (index * TOK_DEV).astype(jnp.int32)
        q_blk = lax.dynamic_slice_in_dim(query_sequence, start, TOK_DEV, 0).astype(jnp.float32)
        g_blk = lax.dynamic_slice_in_dim(output_gradient_sequence, start, TOK_DEV, 0).astype(jnp.float32)
        k_blk = lax.dynamic_slice_in_dim(k_pad, start, window, 0).astype(jnp.float32)
        v_blk = lax.dynamic_slice_in_dim(v_pad, start, window, 0).astype(jnp.float32)
        key_pos = lax.dynamic_slice_in_dim(pos_pad, start, window, 0)
        key_seg = lax.dynamic_slice_in_dim(seg_pad, start, window, 0)
        query_pos = start + jnp.arange(TOK_DEV, dtype=jnp.int32)
        query_seg = lax.dynamic_slice_in_dim(seg_ids.astype(jnp.int32), start, TOK_DEV, 0)
        allowed = (key_seg[None, :] == query_seg[:, None]) & (key_pos[None, :] <= query_pos[:, None])
        scores = score_scale * jnp.einsum("rgd,kd->grk", q_blk, k_blk)
        row_max = jnp.max(jnp.where(allowed, scores, masked_score), axis=-1)
        lse = row_max + jnp.log(jnp.sum(jnp.where(allowed, jnp.exp(scores - row_max[..., None]), 0.0), axis=-1))
        probs = jnp.where(allowed, jnp.exp(scores - lse[..., None]), 0.0)
        probs_b = probs.astype(jnp.bfloat16)
        out_blk = jnp.einsum("grk,kd->rgd", probs_b.astype(jnp.float32), v_blk).astype(jnp.bfloat16)
        row_delta = jnp.sum(g_blk * out_blk.astype(jnp.float32), axis=-1)
        dprob = jnp.einsum("rgd,kd->grk", g_blk, v_blk)
        dscore = (score_scale * probs * (dprob - row_delta.T[:, :, None])).astype(jnp.bfloat16)
        dq_blk = jnp.einsum("grk,kd->rgd", dscore.astype(jnp.float32), k_blk).astype(jnp.bfloat16)
        dk_win = jnp.einsum("grk,rgd->kd", dscore.astype(jnp.float32), q_blk)
        dv_win = jnp.einsum("grk,rgd->kd", probs_b.astype(jnp.float32), g_blk)
        dk_pad = lax.dynamic_update_slice_in_dim(dk_pad, lax.dynamic_slice_in_dim(dk_pad, start, window, 0) + dk_win, start, 0)
        dv_pad = lax.dynamic_update_slice_in_dim(dv_pad, lax.dynamic_slice_in_dim(dv_pad, start, window, 0) + dv_win, start, 0)
        return (dk_pad, dv_pad), (out_blk, dq_blk)

    start_grads = (jnp.zeros((SEQUENCE_LENGTH + reach_rows, HEAD_SIZE), jnp.float32), jnp.zeros((SEQUENCE_LENGTH + reach_rows, HEAD_SIZE), jnp.float32))
    (dk_pad, dv_pad), (out_blocks, dq_blocks) = lax.scan(block, start_grads, jnp.arange(N_CONTEXT, dtype=jnp.int32))
    output_sequence = out_blocks.reshape(SEQUENCE_LENGTH, QUERY_GROUP, HEAD_SIZE)
    query_gradient_sequence = dq_blocks.reshape(SEQUENCE_LENGTH, QUERY_GROUP, HEAD_SIZE)
    return output_sequence, query_gradient_sequence, dk_pad[reach_rows:].astype(jnp.bfloat16), dv_pad[reach_rows:].astype(jnp.bfloat16)


def attend_items(items):
    return attend(items[0], items[1], items[2], items[3], items[4])


def reference(queries, keys, values, grad_out, doc_lengths, deal_plan):
    query_every = deal_rows(queries, deal_plan)
    key_every = deal_rows(keys, deal_plan)
    value_every = deal_rows(values, deal_plan)
    output_gradient_every = deal_rows(grad_out, deal_plan)
    query_sequence = query_every.reshape(N_DP, SEQUENCE_LENGTH, KEY_VALUE_HEADS, QUERY_GROUP, HEAD_SIZE).transpose(0, 2, 1, 3, 4).reshape(N_DP * KEY_VALUE_HEADS, SEQUENCE_LENGTH, QUERY_GROUP, HEAD_SIZE)
    output_gradient_sequence = output_gradient_every.reshape(N_DP, SEQUENCE_LENGTH, KEY_VALUE_HEADS, QUERY_GROUP, HEAD_SIZE).transpose(0, 2, 1, 3, 4).reshape(N_DP * KEY_VALUE_HEADS, SEQUENCE_LENGTH, QUERY_GROUP, HEAD_SIZE)
    key_sequence = key_every.reshape(N_DP, SEQUENCE_LENGTH, KEY_VALUE_HEADS, HEAD_SIZE).transpose(0, 2, 1, 3).reshape(N_DP * KEY_VALUE_HEADS, SEQUENCE_LENGTH, HEAD_SIZE)
    value_sequence = value_every.reshape(N_DP, SEQUENCE_LENGTH, KEY_VALUE_HEADS, HEAD_SIZE).transpose(0, 2, 1, 3).reshape(N_DP * KEY_VALUE_HEADS, SEQUENCE_LENGTH, HEAD_SIZE)
    bounds = jnp.cumsum(doc_lengths.astype(jnp.int32), axis=1)
    positions = jnp.arange(SEQUENCE_LENGTH, dtype=jnp.int32)
    segment_every = jnp.sum((bounds[:, None, :] <= positions[None, :, None]).astype(jnp.int32), axis=-1)
    segment_replica = jnp.repeat(segment_every, KEY_VALUE_HEADS, axis=0)
    output_sequence, query_gradient_sequence, key_gradient_sequence, value_gradient_sequence = lax.map(attend_items, (query_sequence, key_sequence, value_sequence, output_gradient_sequence, segment_replica))
    attention_output = output_sequence.reshape(N_DP, KEY_VALUE_HEADS, SEQUENCE_LENGTH, QUERY_GROUP, HEAD_SIZE).transpose(0, 2, 1, 3, 4).reshape(N_DP * SEQUENCE_LENGTH, QUERY_HEADS * HEAD_SIZE)
    query_gradient = query_gradient_sequence.reshape(N_DP, KEY_VALUE_HEADS, SEQUENCE_LENGTH, QUERY_GROUP, HEAD_SIZE).transpose(0, 2, 1, 3, 4).reshape(N_DP * SEQUENCE_LENGTH, QUERY_HEADS * HEAD_SIZE)
    key_gradient = key_gradient_sequence.reshape(N_DP, KEY_VALUE_HEADS, SEQUENCE_LENGTH, HEAD_SIZE).transpose(0, 2, 1, 3).reshape(N_DP * SEQUENCE_LENGTH, KEY_VALUE_HEADS * HEAD_SIZE)
    value_gradient = value_gradient_sequence.reshape(N_DP, KEY_VALUE_HEADS, SEQUENCE_LENGTH, HEAD_SIZE).transpose(0, 2, 1, 3).reshape(N_DP * SEQUENCE_LENGTH, KEY_VALUE_HEADS * HEAD_SIZE)
    return attention_output, query_gradient, key_gradient, value_gradient
```

```python
import functools

import jax
import jax.numpy as jnp
from jax import lax
from jax.experimental import pallas as pl
from jax.experimental.pallas import tpu as pltpu
from jax.sharding import PartitionSpec as P

HEAD = 128
QUERY_GROUP = 8
NEARBY = 3
MESH = pl.DeviceIdType.MESH
MASKED = -1e30
SCALE = HEAD ** (-0.5)
LOG2E = 1.4426950408889634

NT = (((1,), (1,)), ((), ()))
NN = (((1,), (0,)), ((), ()))


def dot(a, b, dims):
    return lax.dot_general(a, b, dims, preferred_element_type=jnp.float32)


def kernel(
    n_dp, n_ctx, n_lane, sub,
    q_hbm, k_hbm, v_hbm, g_hbm, lengths, plan_hbm,
    out_hbm, dq_hbm, dk_ref, dv_ref,
    q_in, k_in, v_in, g_in, plan,
    q_send, kv_send, g_send, q_rows, kv_rows, g_rows,
    bias, probs, kt, vt, gt, delta, dqt, part_send, part_recv, dkv_acc, out_buf, dq_buf,
    in_sem, plan_sem, q_sems, kv_sems, g_sems, halo_send, halo_recv, back_send, back_recv, out_sem,
):
    s = lax.axis_index("dp")
    c = lax.axis_index("context")
    t = lax.axis_index("tensor")
    peers = n_dp * n_lane
    me = s * n_lane + t
    tok = peers * sub
    width = QUERY_GROUP * HEAD

    def ctx(by):
        return {"context": lax.rem(c + by + n_ctx, n_ctx)}

    def peer(i):
        r = lax.rem(s + i // n_lane, n_dp)
        lane = lax.rem(t + lax.rem(i, n_lane), n_lane)
        return r, lane

    barrier = pltpu.get_barrier_semaphore()

    def greet(i, carry):
        r, lane = peer(i)
        pl.semaphore_signal(
            barrier, inc=1, device_id={"dp": r, "tensor": lane}, device_id_type=MESH
        )
        return carry

    lax.fori_loop(1, peers, greet, 0)
    for by in (-2, -1, 1, 2):
        pl.semaphore_signal(barrier, inc=1, device_id=ctx(by), device_id_type=MESH)

    plan_copy = pltpu.make_async_copy(plan_hbm.at[s], plan, plan_sem)
    plan_copy.start()
    loads = [
        pltpu.make_async_copy(a, b, in_sem.at[n])
        for n, (a, b) in enumerate(
            ((k_hbm, k_in), (v_hbm, v_in), (q_hbm, q_in), (g_hbm, g_in))
        )
    ]
    for copy in loads:
        copy.start()
    plan_copy.wait()
    for copy in loads:
        copy.wait()

    for r in range(n_dp):
        block = jnp.int32(0)
        for b in range(n_dp):
            block = jnp.where(plan[t, b, c] == r, jnp.int32(b), block)
        k_block = k_in[block]
        v_block = v_in[block]
        for lane in range(n_lane):
            kv_send[r * n_lane + lane, :, 0:HEAD] = k_block[:, lane * HEAD : (lane + 1) * HEAD]
            kv_send[r * n_lane + lane, :, HEAD:] = v_block[:, lane * HEAD : (lane + 1) * HEAD]
        q_block = q_in[block]
        g_block = g_in[block]
        for lane in range(n_lane):
            q_send[r * n_lane + lane] = q_block[:, lane * width : (lane + 1) * width]
            g_send[r * n_lane + lane] = g_block[:, lane * width : (lane + 1) * width]

    p = c * tok + lax.broadcasted_iota(jnp.int32, (1, tok), 1)

    def next_bound(n, carry):
        bound, start = carry
        bound = bound + lengths[s, n]
        return bound, jnp.maximum(start, jnp.where(bound <= p, bound, 0))

    _, start = lax.fori_loop(
        0, lengths.shape[1], next_bound, (jnp.int32(0), jnp.zeros((1, tok), jnp.int32))
    )
    j = (c - (NEARBY - 1)) * tok + lax.broadcasted_iota(jnp.int32, (NEARBY * tok, 1), 0)
    bias[...] = jnp.where((j <= p) & (j >= start), 0.0, MASKED).astype(jnp.float32)

    pl.semaphore_wait(barrier, peers - 1 + 4)

    own = (NEARBY - 1) * tok

    def my_rows(base):
        return pl.ds(pl.multiple_of(base + me * sub, sub), sub)

    def deal(sent, rows, base, sems):
        def one(i, carry):
            r, lane = peer(i)
            pltpu.make_async_remote_copy(
                src_ref=sent.at[r * n_lane + lane],
                dst_ref=rows.at[my_rows(base)],
                send_sem=sems.at[0],
                recv_sem=sems.at[1],
                device_id={"dp": r, "tensor": lane},
                device_id_type=MESH,
            ).start()
            return carry

        lax.fori_loop(1, peers, one, 0)
        pltpu.make_async_copy(sent.at[me], rows.at[my_rows(base)], sems.at[1]).start()

    deal(kv_send, kv_rows, own, kv_sems)
    deal(q_send, q_rows, 0, q_sems)
    deal(g_send, g_rows, 0, g_sems)

    def arrived(rows, sems):
        pltpu.make_async_copy(rows, rows, sems.at[1]).wait()

    own_kv = kv_rows.at[pl.ds(own, tok)]
    arrived(own_kv, kv_sems)
    halo = []
    for d in range(1, NEARBY):
        copy = pltpu.make_async_remote_copy(
            src_ref=own_kv,
            dst_ref=kv_rows.at[pl.ds(own - d * tok, tok)],
            send_sem=halo_send.at[d - 1],
            recv_sem=halo_recv.at[d - 1],
            device_id=ctx(d),
            device_id_type=MESH,
        )
        copy.start()
        halo.append(copy)
    for copy in halo:
        copy.wait()
    kt[...] = kv_rows[:, 0:HEAD].astype(jnp.float32).T.astype(jnp.bfloat16)
    vt[...] = kv_rows[:, HEAD:].astype(jnp.float32).T.astype(jnp.bfloat16)

    arrived(q_rows, q_sems)

    def head(h):
        return pl.ds(pl.multiple_of(h * HEAD, HEAD), HEAD)

    def forward(h, carry):
        scores = dot(kv_rows[:, 0:HEAD], q_rows[:, head(h)], NT) * (SCALE * LOG2E) + bias[...]
        top = jnp.max(scores, axis=0, keepdims=True)
        e = jnp.exp2(scores - top)
        pr = e * (1.0 / jnp.sum(e, axis=0, keepdims=True))
        probs[h] = pr
        o = dot(vt[...], pr.astype(jnp.bfloat16), NN)
        out_buf[:, head(h)] = o.T.astype(jnp.bfloat16)
        return carry

    lax.fori_loop(0, QUERY_GROUP, forward, 0)
    out_copy = pltpu.make_async_copy(out_buf, out_hbm, out_sem.at[0])
    out_copy.start()

    arrived(g_rows, g_sems)

    def turn(h, carry):
        g_f = g_rows[:, head(h)].astype(jnp.float32).T
        o_t = out_buf[:, head(h)].astype(jnp.float32).T
        gt[h] = g_f.astype(jnp.bfloat16)
        delta[h] = jnp.sum(g_f * o_t, axis=0, keepdims=True)
        return carry

    lax.fori_loop(0, QUERY_GROUP, turn, 0)

    def backward(n, h):
        at = pl.ds(n * tok, tok)
        pr = probs[h, at]
        dprob = dot(kv_rows[at, HEAD:], gt[h], NN)
        ds = (SCALE * pr * (dprob - delta[h])).astype(jnp.bfloat16)
        term = dot(kt[:, at], ds, NN)
        dqt[h] = term if n == 0 else dqt[h] + term
        dk = dot(ds, q_rows[:, head(h)], NN)
        dv = dot(pr.astype(jnp.bfloat16), g_rows[:, head(h)], NN)
        return dk, dv

    back = []

    def send_part(n):
        copy = pltpu.make_async_remote_copy(
            src_ref=part_send.at[n],
            dst_ref=part_recv.at[n],
            send_sem=back_send.at[n],
            recv_sem=back_recv.at[n],
            device_id=ctx(n - (NEARBY - 1)),
            device_id_type=MESH,
        )
        copy.start()
        back.append(copy)

    for n in range(NEARBY):
        dk, dv = backward(n, 0)
        dkv_acc[:, 0:HEAD] = dk
        dkv_acc[:, HEAD:] = dv
        if n > 0:
            send_part(n - 1)

        def more(h, carry, n=n):
            dk, dv = backward(n, h)
            dkv_acc[:, 0:HEAD] += dk
            dkv_acc[:, HEAD:] += dv
            if n == NEARBY - 1:
                dq_buf[:, head(h)] = dqt[h].T.astype(jnp.bfloat16)
            return carry

        lax.fori_loop(1, QUERY_GROUP, more, 0)
        if n == NEARBY - 1:
            dq_buf[:, 0:HEAD] = dqt[0].T.astype(jnp.bfloat16)
        else:
            part_send[n] = dkv_acc[...].astype(jnp.bfloat16)

    dq_copy = pltpu.make_async_copy(dq_buf, dq_hbm, out_sem.at[1])
    dq_copy.start()
    for copy in back:
        copy.wait()
    total = dkv_acc[...]
    for n in range(NEARBY - 1):
        total = total + part_recv[n].astype(jnp.float32)
    dk_ref[...] = total[:, 0:HEAD].astype(jnp.bfloat16)
    dv_ref[...] = total[:, HEAD:].astype(jnp.bfloat16)

    for sent, sems in ((kv_send, kv_sems), (q_send, q_sems), (g_send, g_sems)):
        gone = sent.at[pl.ds(0, peers - 1)]
        pltpu.make_async_copy(gone, gone, sems.at[0]).wait()
    out_copy.wait()
    dq_copy.wait()


def solution(mesh):
    n_dp, n_ctx, n_lane = (mesh.shape[a] for a in ("dp", "context", "tensor"))

    def on_device(queries, keys, values, grad_out, doc_lengths, deal_plan):
        rows = queries.shape[0]
        sub = rows // n_dp
        peers = n_dp * n_lane
        tok = peers * sub
        width = QUERY_GROUP * HEAD
        bf, f32 = jnp.bfloat16, jnp.float32
        split = [a.reshape(n_dp, sub, a.shape[1]) for a in (queries, keys, values, grad_out)]
        any_ = pl.BlockSpec(memory_space=pl.ANY)
        vmem = pl.BlockSpec(memory_space=pltpu.VMEM)
        smem = pl.BlockSpec(memory_space=pltpu.SMEM)
        dma = pltpu.SemaphoreType.DMA
        return pl.pallas_call(
            functools.partial(kernel, n_dp, n_ctx, n_lane, sub),
            out_shape=(
                jax.ShapeDtypeStruct((tok, width), bf),
                jax.ShapeDtypeStruct((tok, width), bf),
                jax.ShapeDtypeStruct((tok, HEAD), bf),
                jax.ShapeDtypeStruct((tok, HEAD), bf),
            ),
            in_specs=[any_, any_, any_, any_, smem, any_],
            out_specs=(any_, any_, vmem, vmem),
            scratch_shapes=[
                pltpu.VMEM((n_dp, sub, n_lane * width), bf),
                pltpu.VMEM((n_dp, sub, n_lane * HEAD), bf),
                pltpu.VMEM((n_dp, sub, n_lane * HEAD), bf),
                pltpu.VMEM((n_dp, sub, n_lane * width), bf),
                pltpu.SMEM((n_lane, n_dp, n_ctx), jnp.int32),
                pltpu.VMEM((peers, sub, width), bf),
                pltpu.VMEM((peers, sub, 2 * HEAD), bf),
                pltpu.VMEM((peers, sub, width), bf),
                pltpu.VMEM((tok, width), bf),
                pltpu.VMEM((NEARBY * tok, 2 * HEAD), bf),
                pltpu.VMEM((tok, width), bf),
                pltpu.VMEM((NEARBY * tok, tok), f32),
                pltpu.VMEM((QUERY_GROUP, NEARBY * tok, tok), f32),
                pltpu.VMEM((HEAD, NEARBY * tok), bf),
                pltpu.VMEM((HEAD, NEARBY * tok), bf),
                pltpu.VMEM((QUERY_GROUP, HEAD, tok), bf),
                pltpu.VMEM((QUERY_GROUP, 1, tok), f32),
                pltpu.VMEM((QUERY_GROUP, HEAD, tok), f32),
                pltpu.VMEM((NEARBY - 1, tok, 2 * HEAD), bf),
                pltpu.VMEM((NEARBY - 1, tok, 2 * HEAD), bf),
                pltpu.VMEM((tok, 2 * HEAD), f32),
                pltpu.VMEM((tok, width), bf),
                pltpu.VMEM((tok, width), bf),
                dma((4,)),
                dma,
                dma((2,)),
                dma((2,)),
                dma((2,)),
                dma((NEARBY - 1,)),
                dma((NEARBY - 1,)),
                dma((NEARBY - 1,)),
                dma((NEARBY - 1,)),
                dma((2,)),
            ],
            compiler_params=pltpu.CompilerParams(
                collective_id=0, has_side_effects=True, vmem_limit_bytes=48 * 1024 * 1024
            ),
        )(*split, doc_lengths, deal_plan.transpose(1, 2, 3, 0))

    arriving = P(("dp", "context", "tensor"), None)
    leaving = P(("dp", "context"), "tensor")
    return jax.shard_map(
        on_device,
        mesh=mesh,
        in_specs=(arriving, arriving, arriving, arriving, P(), P()),
        out_specs=(leaving, leaving, leaving, leaving),
        check_vma=False,
    )
```

```python
import functools

import jax
import jax.numpy as jnp
from jax import lax
from jax.experimental import pallas as pl
from jax.experimental.pallas import tpu as pltpu
from jax.sharding import PartitionSpec as P

HEAD = 128
QUERY_GROUP = 8
NEARBY = 3
MESH = pl.DeviceIdType.MESH
MASKED = -1e30
SCALE = HEAD ** (-0.5)
LOG2E = 1.4426950408889634

NT = (((1,), (1,)), ((), ()))
NN = (((1,), (0,)), ((), ()))


def dot(a, b, dims):
    return lax.dot_general(a, b, dims, preferred_element_type=jnp.float32)


def kernel(
    n_dp, n_ctx, n_lane, sub,
    q_hbm, k_hbm, v_hbm, g_hbm, lengths, plan_hbm,
    out_hbm, dq_hbm, dk_ref, dv_ref,
    q_in, k_in, v_in, g_in, plan,
    q_send, kv_send, g_send, q_rows, kv_rows, g_rows,
    bias, probs, kt, vt, gt, delta, dqt, part_send, part_recv, dkv_acc, out_buf, dq_buf,
    in_sem, plan_sem, q_sems, kv_sems, g_sems, halo_send, halo_recv, back_send, back_recv, out_sem,
):
    s = lax.axis_index("dp")
    c = lax.axis_index("context")
    t = lax.axis_index("tensor")
    peers = n_dp * n_lane
    me = s * n_lane + t
    tok = peers * sub
    width = QUERY_GROUP * HEAD

    def ctx(by):
        return {"context": lax.rem(c + by + n_ctx, n_ctx)}

    def peer(i):
        r = lax.rem(s + i // n_lane, n_dp)
        lane = lax.rem(t + lax.rem(i, n_lane), n_lane)
        return r, lane

    barrier = pltpu.get_barrier_semaphore()

    def greet(i, carry):
        r, lane = peer(i)
        pl.semaphore_signal(
            barrier, inc=1, device_id={"dp": r, "tensor": lane}, device_id_type=MESH
        )
        return carry

    lax.fori_loop(1, peers, greet, 0)
    for by in (-2, -1, 1, 2):
        pl.semaphore_signal(barrier, inc=1, device_id=ctx(by), device_id_type=MESH)

    plan_copy = pltpu.make_async_copy(plan_hbm.at[s], plan, plan_sem)
    plan_copy.start()
    loads = [
        pltpu.make_async_copy(a, b, in_sem.at[n])
        for n, (a, b) in enumerate(
            ((k_hbm, k_in), (v_hbm, v_in), (q_hbm, q_in), (g_hbm, g_in))
        )
    ]
    for copy in loads:
        copy.start()
    plan_copy.wait()
    for copy in loads:
        copy.wait()

    for r in range(n_dp):
        block = jnp.int32(0)
        for b in range(n_dp):
            block = jnp.where(plan[t, b, c] == r, jnp.int32(b), block)
        k_block = k_in[block]
        v_block = v_in[block]
        for lane in range(n_lane):
            kv_send[r * n_lane + lane, :, 0:HEAD] = k_block[:, lane * HEAD : (lane + 1) * HEAD]
            kv_send[r * n_lane + lane, :, HEAD:] = v_block[:, lane * HEAD : (lane + 1) * HEAD]
        q_block = q_in[block]
        g_block = g_in[block]
        for lane in range(n_lane):
            q_send[r * n_lane + lane] = q_block[:, lane * width : (lane + 1) * width]
            g_send[r * n_lane + lane] = g_block[:, lane * width : (lane + 1) * width]

    p = c * tok + lax.broadcasted_iota(jnp.int32, (1, tok), 1)

    def next_bound(n, carry):
        bound, start = carry
        bound = bound + lengths[s, n]
        return bound, jnp.maximum(start, jnp.where(bound <= p, bound, 0))

    _, start = lax.fori_loop(
        0, lengths.shape[1], next_bound, (jnp.int32(0), jnp.zeros((1, tok), jnp.int32))
    )
    j = (c - (NEARBY - 1)) * tok + lax.broadcasted_iota(jnp.int32, (NEARBY * tok, 1), 0)
    bias[...] = jnp.where((j <= p) & (j >= start), 0.0, MASKED).astype(jnp.float32)

    pl.semaphore_wait(barrier, peers - 1 + 4)

    own = (NEARBY - 1) * tok

    def my_rows(base):
        return pl.ds(pl.multiple_of(base + me * sub, sub), sub)

    def deal(sent, rows, base, sems):
        def one(i, carry):
            r, lane = peer(i)
            pltpu.make_async_remote_copy(
                src_ref=sent.at[r * n_lane + lane],
                dst_ref=rows.at[my_rows(base)],
                send_sem=sems.at[0],
                recv_sem=sems.at[1],
                device_id={"dp": r, "tensor": lane},
                device_id_type=MESH,
            ).start()
            return carry

        lax.fori_loop(1, peers, one, 0)
        pltpu.make_async_copy(sent.at[me], rows.at[my_rows(base)], sems.at[1]).start()

    deal(kv_send, kv_rows, own, kv_sems)
    deal(q_send, q_rows, 0, q_sems)
    deal(g_send, g_rows, 0, g_sems)

    def arrived(rows, sems):
        pltpu.make_async_copy(rows, rows, sems.at[1]).wait()

    own_kv = kv_rows.at[pl.ds(own, tok)]
    arrived(own_kv, kv_sems)
    halo = []
    for d in range(1, NEARBY):
        copy = pltpu.make_async_remote_copy(
            src_ref=own_kv,
            dst_ref=kv_rows.at[pl.ds(own - d * tok, tok)],
            send_sem=halo_send.at[d - 1],
            recv_sem=halo_recv.at[d - 1],
            device_id=ctx(d),
            device_id_type=MESH,
        )
        copy.start()
        halo.append(copy)
    for copy in halo:
        copy.wait()
    kt[...] = kv_rows[:, 0:HEAD].astype(jnp.float32).T.astype(jnp.bfloat16)
    vt[...] = kv_rows[:, HEAD:].astype(jnp.float32).T.astype(jnp.bfloat16)

    arrived(q_rows, q_sems)

    def head(h):
        return pl.ds(pl.multiple_of(h * HEAD, HEAD), HEAD)

    def forward(h, carry):
        scores = dot(kv_rows[:, 0:HEAD], q_rows[:, head(h)], NT) * (SCALE * LOG2E) + bias[...]
        top = jnp.max(scores, axis=0, keepdims=True)
        e = jnp.exp2(scores - top)
        pr = e * (1.0 / jnp.sum(e, axis=0, keepdims=True))
        probs[h] = pr
        o = dot(vt[...], pr.astype(jnp.bfloat16), NN)
        out_buf[:, head(h)] = o.T.astype(jnp.bfloat16)
        return carry

    lax.fori_loop(0, QUERY_GROUP, forward, 0)
    out_copy = pltpu.make_async_copy(out_buf, out_hbm, out_sem.at[0])
    out_copy.start()

    arrived(g_rows, g_sems)

    def turn(h, carry):
        g_f = g_rows[:, head(h)].astype(jnp.float32).T
        o_t = out_buf[:, head(h)].astype(jnp.float32).T
        gt[h] = g_f.astype(jnp.bfloat16)
        delta[h] = jnp.sum(g_f * o_t, axis=0, keepdims=True)
        return carry

    lax.fori_loop(0, QUERY_GROUP, turn, 0)

    def backward(n, h):
        at = pl.ds(n * tok, tok)
        pr = probs[h, at]
        dprob = dot(kv_rows[at, HEAD:], gt[h], NN)
        ds = (SCALE * pr * (dprob - delta[h])).astype(jnp.bfloat16)
        term = dot(kt[:, at], ds, NN)
        dqt[h] = term if n == 0 else dqt[h] + term
        dk = dot(ds, q_rows[:, head(h)], NN)
        dv = dot(pr.astype(jnp.bfloat16), g_rows[:, head(h)], NN)
        return dk, dv

    back = []

    def send_part(n):
        copy = pltpu.make_async_remote_copy(
            src_ref=part_send.at[n],
            dst_ref=part_recv.at[n],
            send_sem=back_send.at[n],
            recv_sem=back_recv.at[n],
            device_id=ctx(n - (NEARBY - 1)),
            device_id_type=MESH,
        )
        copy.start()
        back.append(copy)

    for n in range(NEARBY):
        dk, dv = backward(n, 0)
        dkv_acc[:, 0:HEAD] = dk
        dkv_acc[:, HEAD:] = dv
        if n > 0:
            send_part(n - 1)

        def more(h, carry, n=n):
            dk, dv = backward(n, h)
            dkv_acc[:, 0:HEAD] += dk
            dkv_acc[:, HEAD:] += dv
            if n == NEARBY - 1:
                dq_buf[:, head(h)] = dqt[h].T.astype(jnp.bfloat16)
            return carry

        lax.fori_loop(1, QUERY_GROUP, more, 0)
        if n == NEARBY - 1:
            dq_buf[:, 0:HEAD] = dqt[0].T.astype(jnp.bfloat16)
        else:
            part_send[n] = dkv_acc[...].astype(jnp.bfloat16)

    dq_copy = pltpu.make_async_copy(dq_buf, dq_hbm, out_sem.at[1])
    dq_copy.start()
    for copy in back:
        copy.wait()
    total = dkv_acc[...]
    for n in range(NEARBY - 1):
        total = total + part_recv[n].astype(jnp.float32)
    dk_ref[...] = total[:, 0:HEAD].astype(jnp.bfloat16)
    dv_ref[...] = total[:, HEAD:].astype(jnp.bfloat16)

    for sent, sems in ((kv_send, kv_sems), (q_send, q_sems), (g_send, g_sems)):
        gone = sent.at[pl.ds(0, peers - 1)]
        pltpu.make_async_copy(gone, gone, sems.at[0]).wait()
    out_copy.wait()
    dq_copy.wait()


def store(*refs):
    sems = refs[8]
    copies = [pltpu.make_async_copy(refs[n], refs[n + 4], sems.at[n]) for n in range(4)]
    for copy in copies:
        copy.start()
    for copy in copies:
        copy.wait()


def solution(mesh):
    n_dp, n_ctx, n_lane = (mesh.shape[a] for a in ("dp", "context", "tensor"))

    def on_device(queries, keys, values, grad_out, doc_lengths, deal_plan):
        rows = queries.shape[0]
        sub = rows // n_dp
        peers = n_dp * n_lane
        tok = peers * sub
        width = QUERY_GROUP * HEAD
        bf, f32 = jnp.bfloat16, jnp.float32
        split = [
            pltpu.with_memory_space_constraint(a.reshape(n_dp, sub, a.shape[1]), pltpu.HBM)
            for a in (queries, keys, values, grad_out)
        ]
        plans = pltpu.with_memory_space_constraint(deal_plan.transpose(1, 2, 3, 0), pltpu.HBM)
        any_ = pl.BlockSpec(memory_space=pl.ANY)
        hbm = pl.BlockSpec(memory_space=pltpu.HBM)
        vmem = pl.BlockSpec(memory_space=pltpu.VMEM)
        smem = pl.BlockSpec(memory_space=pltpu.SMEM)
        dma = pltpu.SemaphoreType.DMA
        results = pl.pallas_call(
            functools.partial(kernel, n_dp, n_ctx, n_lane, sub),
            out_shape=(
                pltpu.VMEM((tok, width), bf),
                pltpu.VMEM((tok, width), bf),
                pltpu.VMEM((tok, HEAD), bf),
                pltpu.VMEM((tok, HEAD), bf),
            ),
            in_specs=[hbm, hbm, hbm, hbm, smem, hbm],
            out_specs=(any_, any_, vmem, vmem),
            scratch_shapes=[
                pltpu.VMEM((n_dp, sub, n_lane * width), bf),
                pltpu.VMEM((n_dp, sub, n_lane * HEAD), bf),
                pltpu.VMEM((n_dp, sub, n_lane * HEAD), bf),
                pltpu.VMEM((n_dp, sub, n_lane * width), bf),
                pltpu.SMEM((n_lane, n_dp, n_ctx), jnp.int32),
                pltpu.VMEM((peers, sub, width), bf),
                pltpu.VMEM((peers, sub, 2 * HEAD), bf),
                pltpu.VMEM((peers, sub, width), bf),
                pltpu.VMEM((tok, width), bf),
                pltpu.VMEM((NEARBY * tok, 2 * HEAD), bf),
                pltpu.VMEM((tok, width), bf),
                pltpu.VMEM((NEARBY * tok, tok), f32),
                pltpu.VMEM((QUERY_GROUP, NEARBY * tok, tok), f32),
                pltpu.VMEM((HEAD, NEARBY * tok), bf),
                pltpu.VMEM((HEAD, NEARBY * tok), bf),
                pltpu.VMEM((QUERY_GROUP, HEAD, tok), bf),
                pltpu.VMEM((QUERY_GROUP, 1, tok), f32),
                pltpu.VMEM((QUERY_GROUP, HEAD, tok), f32),
                pltpu.VMEM((NEARBY - 1, tok, 2 * HEAD), bf),
                pltpu.VMEM((NEARBY - 1, tok, 2 * HEAD), bf),
                pltpu.VMEM((tok, 2 * HEAD), f32),
                pltpu.VMEM((tok, width), bf),
                pltpu.VMEM((tok, width), bf),
                dma((4,)),
                dma,
                dma((2,)),
                dma((2,)),
                dma((2,)),
                dma((NEARBY - 1,)),
                dma((NEARBY - 1,)),
                dma((NEARBY - 1,)),
                dma((NEARBY - 1,)),
                dma((2,)),
            ],
            compiler_params=pltpu.CompilerParams(
                collective_id=0, has_side_effects=True, vmem_limit_bytes=48 * 1024 * 1024
            ),
        )(*split, doc_lengths, plans)
        return pl.pallas_call(
            store,
            out_shape=tuple(pltpu.HBM(a.shape, a.dtype) for a in results),
            in_specs=[vmem] * 4,
            out_specs=(hbm,) * 4,
            scratch_shapes=[dma((4,))],
        )(*[pltpu.with_memory_space_constraint(a, pltpu.VMEM) for a in results])

    arriving = P(("dp", "context", "tensor"), None)
    leaving = P(("dp", "context"), "tensor")
    return jax.shard_map(
        on_device,
        mesh=mesh,
        in_specs=(arriving, arriving, arriving, arriving, P(), P()),
        out_specs=(leaving, leaving, leaving, leaving),
        check_vma=False,
    )
```

```python
import functools

import jax
import jax.numpy as jnp
from jax import lax
from jax.experimental import pallas as pl
from jax.experimental.pallas import tpu as pltpu
from jax.sharding import PartitionSpec as P

HEAD = 128
QUERY_GROUP = 8
NEARBY = 3
MESH = pl.DeviceIdType.MESH
GROUPS = ((0, 4), (4, 6), (6, 8))
MASKED = -1e30
SCALE = HEAD ** (-0.5)
LOG2E = 1.4426950408889634

NT = (((1,), (1,)), ((), ()))
NN = (((1,), (0,)), ((), ()))


def dot(a, b, dims):
    return lax.dot_general(a, b, dims, preferred_element_type=jnp.float32)


def kernel(
    n_dp, n_ctx, n_lane, sub,
    q_hbm, k_hbm, v_hbm, g_hbm, lengths, plan_hbm,
    out_hbm, dq_hbm, dk_ref, dv_ref,
    q_in, k_in, v_in, g_in, plan,
    q_send, kv_send, g_send, q_rows, kv_rows, g_rows,
    bias, probs, kt, vt, gt, delta, dqt, part_send, part_recv, dkv_acc, out_buf, dq_buf,
    in_sem, plan_sem, q_sems, kv_sems, g_sems, halo_send, halo_recv, back_send, back_recv, out_sem,
):
    s = lax.axis_index("dp")
    c = lax.axis_index("context")
    t = lax.axis_index("tensor")
    peers = n_dp * n_lane
    me = s * n_lane + t
    tok = peers * sub
    width = QUERY_GROUP * HEAD

    def ctx(by):
        return {"context": lax.rem(c + by + n_ctx, n_ctx)}

    def peer(i):
        r = lax.rem(s + i // n_lane, n_dp)
        lane = lax.rem(t + lax.rem(i, n_lane), n_lane)
        return r, lane

    barrier = pltpu.get_barrier_semaphore()

    def greet(i, carry):
        r, lane = peer(i)
        pl.semaphore_signal(
            barrier, inc=1, device_id={"dp": r, "tensor": lane}, device_id_type=MESH
        )
        return carry

    lax.fori_loop(1, peers, greet, 0)
    for by in (-2, -1, 1, 2):
        pl.semaphore_signal(barrier, inc=1, device_id=ctx(by), device_id_type=MESH)

    plan_copy = pltpu.make_async_copy(plan_hbm.at[s], plan, plan_sem)
    plan_copy.start()
    loads = [
        pltpu.make_async_copy(a, b, in_sem.at[n])
        for n, (a, b) in enumerate(
            ((k_hbm, k_in), (v_hbm, v_in), (q_hbm, q_in), (g_hbm, g_in))
        )
    ]
    for copy in loads:
        copy.start()
    plan_copy.wait()
    for copy in loads:
        copy.wait()

    for r in range(n_dp):
        block = jnp.int32(0)
        for b in range(n_dp):
            block = jnp.where(plan[t, b, c] == r, jnp.int32(b), block)
        k_block = k_in[block]
        v_block = v_in[block]
        for lane in range(n_lane):
            kv_send[r * n_lane + lane, :, 0:HEAD] = k_block[:, lane * HEAD : (lane + 1) * HEAD]
            kv_send[r * n_lane + lane, :, HEAD:] = v_block[:, lane * HEAD : (lane + 1) * HEAD]
        q_block = q_in[block]
        g_block = g_in[block]
        for lane in range(n_lane):
            q_send[r * n_lane + lane] = q_block[:, lane * width : (lane + 1) * width]
            g_send[r * n_lane + lane] = g_block[:, lane * width : (lane + 1) * width]

    p = c * tok + lax.broadcasted_iota(jnp.int32, (1, tok), 1)

    def next_bound(n, carry):
        bound, start = carry
        bound = bound + lengths[s, n]
        return bound, jnp.maximum(start, jnp.where(bound <= p, bound, 0))

    _, start = lax.fori_loop(
        0, lengths.shape[1], next_bound, (jnp.int32(0), jnp.zeros((1, tok), jnp.int32))
    )
    j = (c - (NEARBY - 1)) * tok + lax.broadcasted_iota(jnp.int32, (NEARBY * tok, 1), 0)
    bias[...] = jnp.where((j <= p) & (j >= start), 0.0, MASKED).astype(jnp.float32)

    pl.semaphore_wait(barrier, peers - 1 + 4)

    own = (NEARBY - 1) * tok

    def my_rows(base):
        return pl.ds(pl.multiple_of(base + me * sub, sub), sub)

    def deal(sent, rows, base, sems, cols):
        def one(i, carry):
            r, lane = peer(i)
            pltpu.make_async_remote_copy(
                src_ref=sent.at[r * n_lane + lane, :, cols],
                dst_ref=rows.at[my_rows(base), cols],
                send_sem=sems.at[0],
                recv_sem=sems.at[1],
                device_id={"dp": r, "tensor": lane},
                device_id_type=MESH,
            ).start()
            return carry

        lax.fori_loop(1, peers, one, 0)
        pltpu.make_async_copy(
            sent.at[me, :, cols], rows.at[my_rows(base), cols], sems.at[1]
        ).start()

    def columns(group):
        return pl.ds(group[0] * HEAD, (group[1] - group[0]) * HEAD)

    def arrived(rows, sems):
        pltpu.make_async_copy(rows, rows, sems.at[1]).wait()

    deals = [
        (kv_send, kv_rows, own, kv_sems, pl.ds(0, 2 * HEAD)),
        (q_send, q_rows, 0, q_sems, pl.ds(0, width)),
    ]
    for n, group in enumerate(GROUPS):
        deals.append((g_send, g_rows, 0, g_sems.at[n], columns(group)))
    for one_deal in deals:
        deal(*one_deal)

    own_kv = kv_rows.at[pl.ds(own, tok)]
    arrived(own_kv, kv_sems)
    halo = []
    for d in range(1, NEARBY):
        copy = pltpu.make_async_remote_copy(
            src_ref=own_kv,
            dst_ref=kv_rows.at[pl.ds(own - d * tok, tok)],
            send_sem=halo_send.at[d - 1],
            recv_sem=halo_recv.at[d - 1],
            device_id=ctx(d),
            device_id_type=MESH,
        )
        copy.start()
        halo.append(copy)
    for copy in halo:
        copy.wait()
    kt[...] = kv_rows[:, 0:HEAD].astype(jnp.float32).T.astype(jnp.bfloat16)
    vt[...] = kv_rows[:, HEAD:].astype(jnp.float32).T.astype(jnp.bfloat16)

    arrived(q_rows, q_sems)

    def head(h):
        return pl.ds(pl.multiple_of(h * HEAD, HEAD), HEAD)

    def forward(h, carry):
        scores = dot(kv_rows[:, 0:HEAD], q_rows[:, head(h)], NT) * (SCALE * LOG2E) + bias[...]
        top = jnp.max(scores, axis=0, keepdims=True)
        e = jnp.exp2(scores - top)
        pr = e * (1.0 / jnp.sum(e, axis=0, keepdims=True))
        probs[h] = pr
        o = dot(vt[...], pr.astype(jnp.bfloat16), NN)
        out_buf[:, head(h)] = o.T.astype(jnp.bfloat16)
        return carry

    dkv_acc[...] = jnp.zeros_like(dkv_acc)
    lax.fori_loop(0, QUERY_GROUP, forward, 0)
    out_copy = pltpu.make_async_copy(out_buf, out_hbm, out_sem.at[0])
    out_copy.start()

    def turn(h):
        g_f = g_rows[:, head(h)].astype(jnp.float32).T
        o_t = out_buf[:, head(h)].astype(jnp.float32).T
        gt[h] = g_f.astype(jnp.bfloat16)
        delta[h] = jnp.sum(g_f * o_t, axis=0, keepdims=True)

    def backward(n, h):
        at = pl.ds(n * tok, tok)
        pr = probs[h, at]
        dprob = dot(kv_rows[at, HEAD:], gt[h], NN)
        ds = (SCALE * pr * (dprob - delta[h])).astype(jnp.bfloat16)
        term = dot(kt[:, at], ds, NN)
        total = term if n == 0 else dqt[h] + term
        if n == NEARBY - 1:
            dq_buf[:, head(h)] = total.T.astype(jnp.bfloat16)
        else:
            dqt[h] = total
        dkv_acc[at, 0:HEAD] += dot(ds, q_rows[:, head(h)], NN)
        dkv_acc[at, HEAD:] += dot(pr.astype(jnp.bfloat16), g_rows[:, head(h)], NN)

    back = []

    def send_part(n):
        copy = pltpu.make_async_remote_copy(
            src_ref=part_send.at[n],
            dst_ref=part_recv.at[n],
            send_sem=back_send.at[n],
            recv_sem=back_recv.at[n],
            device_id=ctx(n - (NEARBY - 1)),
            device_id_type=MESH,
        )
        copy.start()
        back.append(copy)

    for n, group in enumerate(GROUPS[:-1]):
        arrived(g_rows.at[:, columns(group)], g_sems.at[n])

        def whole(h, carry):
            turn(h)
            for m in range(NEARBY):
                backward(m, h)
            return carry

        lax.fori_loop(*group, whole, 0)

    first, end = GROUPS[-1]
    arrived(g_rows.at[:, columns(GROUPS[-1])], g_sems.at[len(GROUPS) - 1])
    for h in range(first, end):
        turn(h)
    for m in range(NEARBY):
        for h in range(first, end):
            backward(m, h)
            if h == first and m > 0:
                send_part(m - 1)
        if m < NEARBY - 1:
            part_send[m] = dkv_acc[m * tok : (m + 1) * tok].astype(jnp.bfloat16)

    dq_copy = pltpu.make_async_copy(dq_buf, dq_hbm, out_sem.at[1])
    dq_copy.start()
    for copy in back:
        copy.wait()
    total = dkv_acc[own:]
    for n in range(NEARBY - 1):
        total = total + part_recv[n].astype(jnp.float32)
    dk_ref[...] = total[:, 0:HEAD].astype(jnp.bfloat16)
    dv_ref[...] = total[:, HEAD:].astype(jnp.bfloat16)

    for sent, _, _, sems, cols in deals:
        gone = sent.at[pl.ds(0, peers - 1), :, cols]
        pltpu.make_async_copy(gone, gone, sems.at[0]).wait()
    out_copy.wait()
    dq_copy.wait()


def store(*refs):
    sems = refs[8]
    copies = [pltpu.make_async_copy(refs[n], refs[n + 4], sems.at[n]) for n in range(4)]
    for copy in copies:
        copy.start()
    for copy in copies:
        copy.wait()


def solution(mesh):
    n_dp, n_ctx, n_lane = (mesh.shape[a] for a in ("dp", "context", "tensor"))

    def on_device(queries, keys, values, grad_out, doc_lengths, deal_plan):
        rows = queries.shape[0]
        sub = rows // n_dp
        peers = n_dp * n_lane
        tok = peers * sub
        width = QUERY_GROUP * HEAD
        bf, f32 = jnp.bfloat16, jnp.float32
        split = [
            pltpu.with_memory_space_constraint(a.reshape(n_dp, sub, a.shape[1]), pltpu.HBM)
            for a in (queries, keys, values, grad_out)
        ]
        plans = pltpu.with_memory_space_constraint(deal_plan.transpose(1, 2, 3, 0), pltpu.HBM)
        any_ = pl.BlockSpec(memory_space=pl.ANY)
        hbm = pl.BlockSpec(memory_space=pltpu.HBM)
        vmem = pl.BlockSpec(memory_space=pltpu.VMEM)
        smem = pl.BlockSpec(memory_space=pltpu.SMEM)
        dma = pltpu.SemaphoreType.DMA
        results = pl.pallas_call(
            functools.partial(kernel, n_dp, n_ctx, n_lane, sub),
            out_shape=(
                pltpu.VMEM((tok, width), bf),
                pltpu.VMEM((tok, width), bf),
                pltpu.VMEM((tok, HEAD), bf),
                pltpu.VMEM((tok, HEAD), bf),
            ),
            in_specs=[hbm, hbm, hbm, hbm, smem, hbm],
            out_specs=(any_, any_, vmem, vmem),
            scratch_shapes=[
                pltpu.VMEM((n_dp, sub, n_lane * width), bf),
                pltpu.VMEM((n_dp, sub, n_lane * HEAD), bf),
                pltpu.VMEM((n_dp, sub, n_lane * HEAD), bf),
                pltpu.VMEM((n_dp, sub, n_lane * width), bf),
                pltpu.SMEM((n_lane, n_dp, n_ctx), jnp.int32),
                pltpu.VMEM((peers, sub, width), bf),
                pltpu.VMEM((peers, sub, 2 * HEAD), bf),
                pltpu.VMEM((peers, sub, width), bf),
                pltpu.VMEM((tok, width), bf),
                pltpu.VMEM((NEARBY * tok, 2 * HEAD), bf),
                pltpu.VMEM((tok, width), bf),
                pltpu.VMEM((NEARBY * tok, tok), f32),
                pltpu.VMEM((QUERY_GROUP, NEARBY * tok, tok), f32),
                pltpu.VMEM((HEAD, NEARBY * tok), bf),
                pltpu.VMEM((HEAD, NEARBY * tok), bf),
                pltpu.VMEM((QUERY_GROUP, HEAD, tok), bf),
                pltpu.VMEM((QUERY_GROUP, 1, tok), f32),
                pltpu.VMEM((QUERY_GROUP, HEAD, tok), f32),
                pltpu.VMEM((NEARBY - 1, tok, 2 * HEAD), bf),
                pltpu.VMEM((NEARBY - 1, tok, 2 * HEAD), bf),
                pltpu.VMEM((NEARBY * tok, 2 * HEAD), f32),
                pltpu.VMEM((tok, width), bf),
                pltpu.VMEM((tok, width), bf),
                dma((4,)),
                dma,
                dma((2,)),
                dma((2,)),
                dma((len(GROUPS), 2)),
                dma((NEARBY - 1,)),
                dma((NEARBY - 1,)),
                dma((NEARBY - 1,)),
                dma((NEARBY - 1,)),
                dma((2,)),
            ],
            compiler_params=pltpu.CompilerParams(
                collective_id=0, has_side_effects=True, vmem_limit_bytes=48 * 1024 * 1024
            ),
        )(*split, doc_lengths, plans)
        return pl.pallas_call(
            store,
            out_shape=tuple(pltpu.HBM(a.shape, a.dtype) for a in results),
            in_specs=[vmem] * 4,
            out_specs=(hbm,) * 4,
            scratch_shapes=[dma((4,))],
        )(*[pltpu.with_memory_space_constraint(a, pltpu.VMEM) for a in results])

    arriving = P(("dp", "context", "tensor"), None)
    leaving = P(("dp", "context"), "tensor")
    return jax.shard_map(
        on_device,
        mesh=mesh,
        in_specs=(arriving, arriving, arriving, arriving, P(), P()),
        out_specs=(leaving, leaving, leaving, leaving),
        check_vma=False,
    )
```

```python
import functools

import jax
import jax.numpy as jnp
from jax import lax
from jax.experimental import pallas as pl
from jax.experimental.pallas import tpu as pltpu
from jax.sharding import PartitionSpec as P

HEAD = 128
QUERY_GROUP = 8
NEARBY = 3
MESH = pl.DeviceIdType.MESH
Q_GROUPS = ((0, 4), (4, 8))
G_GROUPS = ((0, 4), (4, 7), (7, 8))
MASKED = -1e30
SCALE = HEAD ** (-0.5)
LOG2E = 1.4426950408889634

NT = (((1,), (1,)), ((), ()))
NN = (((1,), (0,)), ((), ()))


def dot(a, b, dims):
    return lax.dot_general(a, b, dims, preferred_element_type=jnp.float32)


def kernel(
    n_dp, n_ctx, n_lane, sub,
    q_hbm, k_hbm, v_hbm, g_hbm, lengths_hbm, plan_hbm,
    out_hbm, dq_hbm, dk_ref, dv_ref,
    q_in, k_in, v_in, g_in, lengths, plan,
    q_send, kv_send, g_send, q_rows, kv_rows, g_rows,
    bias, probs, kt, vt, gt, delta, dqt, part_send, part_recv, dkv_acc, out_buf, dq_buf,
    in_sem, plan_sem, q_sems, kv_sems, g_sems, halo_send, halo_recv, back_send, back_recv, out_sem,
):
    s = lax.axis_index("dp")
    c = lax.axis_index("context")
    t = lax.axis_index("tensor")
    peers = n_dp * n_lane
    me = s * n_lane + t
    tok = peers * sub
    width = QUERY_GROUP * HEAD

    def ctx(by):
        return {"context": lax.rem(c + by + n_ctx, n_ctx)}

    def peer(i):
        r = lax.rem(s + i // n_lane, n_dp)
        lane = lax.rem(t + lax.rem(i, n_lane), n_lane)
        return r, lane

    barrier = pltpu.get_barrier_semaphore()

    def greet(i, carry):
        r, lane = peer(i)
        pl.semaphore_signal(
            barrier, inc=1, device_id={"dp": r, "tensor": lane}, device_id_type=MESH
        )
        return carry

    lax.fori_loop(1, peers, greet, 0)
    for by in (-2, -1, 1, 2):
        pl.semaphore_signal(barrier, inc=1, device_id=ctx(by), device_id_type=MESH)

    plan_copy = pltpu.make_async_copy(plan_hbm.at[s], plan, plan_sem.at[0])
    plan_copy.start()
    lengths_copy = pltpu.make_async_copy(lengths_hbm, lengths, plan_sem.at[1])
    lengths_copy.start()
    loads = [
        pltpu.make_async_copy(a, b, in_sem.at[n])
        for n, (a, b) in enumerate(
            ((k_hbm, k_in), (v_hbm, v_in), (q_hbm, q_in), (g_hbm, g_in))
        )
    ]
    for copy in loads:
        copy.start()
    plan_copy.wait()
    lengths_copy.wait()
    for copy in loads:
        copy.wait()

    for r in range(n_dp):
        block = jnp.int32(0)
        for b in range(n_dp):
            block = jnp.where(plan[t, b, c] == r, jnp.int32(b), block)
        k_block = k_in[block]
        v_block = v_in[block]
        for lane in range(n_lane):
            kv_send[r * n_lane + lane, :, 0:HEAD] = k_block[:, lane * HEAD : (lane + 1) * HEAD]
            kv_send[r * n_lane + lane, :, HEAD:] = v_block[:, lane * HEAD : (lane + 1) * HEAD]
        q_block = q_in[block]
        g_block = g_in[block]
        for lane in range(n_lane):
            q_send[r * n_lane + lane] = q_block[:, lane * width : (lane + 1) * width]
            g_send[r * n_lane + lane] = g_block[:, lane * width : (lane + 1) * width]

    p = c * tok + lax.broadcasted_iota(jnp.int32, (1, tok), 1)

    def next_bound(n, carry):
        bound, start = carry
        bound = bound + lengths[s, n]
        return bound, jnp.maximum(start, jnp.where(bound <= p, bound, 0))

    _, start = lax.fori_loop(
        0, lengths.shape[1], next_bound, (jnp.int32(0), jnp.zeros((1, tok), jnp.int32))
    )
    j = (c - (NEARBY - 1)) * tok + lax.broadcasted_iota(jnp.int32, (NEARBY * tok, 1), 0)
    bias[...] = jnp.where((j <= p) & (j >= start), 0.0, MASKED).astype(jnp.float32)

    pl.semaphore_wait(barrier, peers - 1 + 4)

    own = (NEARBY - 1) * tok

    def my_rows(base):
        return pl.ds(pl.multiple_of(base + me * sub, sub), sub)

    def deal(sent, rows, base, sems, cols):
        def one(i, carry):
            r, lane = peer(i)
            pltpu.make_async_remote_copy(
                src_ref=sent.at[r * n_lane + lane, :, cols],
                dst_ref=rows.at[my_rows(base), cols],
                send_sem=sems.at[0],
                recv_sem=sems.at[1],
                device_id={"dp": r, "tensor": lane},
                device_id_type=MESH,
            ).start()
            return carry

        lax.fori_loop(1, peers, one, 0)
        pltpu.make_async_copy(
            sent.at[me, :, cols], rows.at[my_rows(base), cols], sems.at[1]
        ).start()

    def columns(group):
        return pl.ds(group[0] * HEAD, (group[1] - group[0]) * HEAD)

    def arrived(rows, sems):
        pltpu.make_async_copy(rows, rows, sems.at[1]).wait()

    deals = [
        (kv_send, kv_rows, own, kv_sems, pl.ds(0, 2 * HEAD)),
    ]
    for n, group in enumerate(Q_GROUPS):
        deals.append((q_send, q_rows, 0, q_sems.at[n], columns(group)))
    for n, group in enumerate(G_GROUPS):
        deals.append((g_send, g_rows, 0, g_sems.at[n], columns(group)))
    for one_deal in deals:
        deal(*one_deal)

    own_kv = kv_rows.at[pl.ds(own, tok)]
    arrived(own_kv, kv_sems)
    halo = []
    for d in range(1, NEARBY):
        copy = pltpu.make_async_remote_copy(
            src_ref=own_kv,
            dst_ref=kv_rows.at[pl.ds(own - d * tok, tok)],
            send_sem=halo_send.at[d - 1],
            recv_sem=halo_recv.at[d - 1],
            device_id=ctx(d),
            device_id_type=MESH,
        )
        copy.start()
        halo.append(copy)
    for copy in halo:
        copy.wait()
    kt[...] = kv_rows[:, 0:HEAD].astype(jnp.float32).T.astype(jnp.bfloat16)
    vt[...] = kv_rows[:, HEAD:].astype(jnp.float32).T.astype(jnp.bfloat16)

    def head(h):
        return pl.ds(pl.multiple_of(h * HEAD, HEAD), HEAD)

    def forward(h, carry):
        scores = dot(kv_rows[:, 0:HEAD], q_rows[:, head(h)], NT) * (SCALE * LOG2E) + bias[...]
        top = jnp.max(scores, axis=0, keepdims=True)
        e = jnp.exp2(scores - top)
        pr = e * (1.0 / jnp.sum(e, axis=0, keepdims=True))
        probs[h] = pr
        o = dot(vt[...], pr.astype(jnp.bfloat16), NN)
        out_buf[:, head(h)] = o.T.astype(jnp.bfloat16)
        return carry

    dkv_acc[...] = jnp.zeros_like(dkv_acc)
    for n, group in enumerate(Q_GROUPS):
        arrived(q_rows.at[:, columns(group)], q_sems.at[n])
        lax.fori_loop(*group, forward, 0)
    out_copy = pltpu.make_async_copy(out_buf, out_hbm, out_sem.at[0])
    out_copy.start()

    def turn(h):
        g_f = g_rows[:, head(h)].astype(jnp.float32).T
        o_t = out_buf[:, head(h)].astype(jnp.float32).T
        gt[h] = g_f.astype(jnp.bfloat16)
        delta[h] = jnp.sum(g_f * o_t, axis=0, keepdims=True)

    def backward(n, h):
        at = pl.ds(n * tok, tok)
        pr = probs[h, at]
        dprob = dot(kv_rows[at, HEAD:], gt[h], NN)
        ds = (SCALE * pr * (dprob - delta[h])).astype(jnp.bfloat16)
        term = dot(kt[:, at], ds, NN)
        total = term if n == 0 else dqt[h] + term
        if n == NEARBY - 1:
            dq_buf[:, head(h)] = total.T.astype(jnp.bfloat16)
        else:
            dqt[h] = total
        dkv_acc[at, 0:HEAD] += dot(ds, q_rows[:, head(h)], NN)
        dkv_acc[at, HEAD:] += dot(pr.astype(jnp.bfloat16), g_rows[:, head(h)], NN)

    back = []

    def send_part(n):
        copy = pltpu.make_async_remote_copy(
            src_ref=part_send.at[n],
            dst_ref=part_recv.at[n],
            send_sem=back_send.at[n],
            recv_sem=back_recv.at[n],
            device_id=ctx(n - (NEARBY - 1)),
            device_id_type=MESH,
        )
        copy.start()
        back.append(copy)

    for n, group in enumerate(G_GROUPS[:-1]):
        arrived(g_rows.at[:, columns(group)], g_sems.at[n])

        def whole(h, carry):
            turn(h)
            for m in range(NEARBY):
                backward(m, h)
            return carry

        lax.fori_loop(*group, whole, 0)

    first, end = G_GROUPS[-1]
    arrived(g_rows.at[:, columns(G_GROUPS[-1])], g_sems.at[len(G_GROUPS) - 1])
    for h in range(first, end):
        turn(h)
    for m in range(NEARBY):
        for h in range(first, end):
            backward(m, h)
            if h == first and m > 0:
                send_part(m - 1)
        if m < NEARBY - 1:
            part_send[m] = dkv_acc[m * tok : (m + 1) * tok].astype(jnp.bfloat16)

    dq_copy = pltpu.make_async_copy(dq_buf, dq_hbm, out_sem.at[1])
    dq_copy.start()
    for copy in back:
        copy.wait()
    total = dkv_acc[own:]
    for n in range(NEARBY - 1):
        total = total + part_recv[n].astype(jnp.float32)
    dk_ref[...] = total[:, 0:HEAD].astype(jnp.bfloat16)
    dv_ref[...] = total[:, HEAD:].astype(jnp.bfloat16)

    for sent, _, _, sems, cols in deals:
        gone = sent.at[pl.ds(0, peers - 1), :, cols]
        pltpu.make_async_copy(gone, gone, sems.at[0]).wait()
    out_copy.wait()
    dq_copy.wait()


def store(*refs):
    sems = refs[8]
    copies = [pltpu.make_async_copy(refs[n], refs[n + 4], sems.at[n]) for n in range(4)]
    for copy in copies:
        copy.start()
    for copy in copies:
        copy.wait()


def solution(mesh):
    n_dp, n_ctx, n_lane = (mesh.shape[a] for a in ("dp", "context", "tensor"))

    def on_device(queries, keys, values, grad_out, doc_lengths, deal_plan):
        rows = queries.shape[0]
        sub = rows // n_dp
        peers = n_dp * n_lane
        tok = peers * sub
        width = QUERY_GROUP * HEAD
        bf, f32 = jnp.bfloat16, jnp.float32
        split = [
            pltpu.with_memory_space_constraint(a.reshape(n_dp, sub, a.shape[1]), pltpu.HBM)
            for a in (queries, keys, values, grad_out)
        ]
        lengths = pltpu.with_memory_space_constraint(doc_lengths, pltpu.HBM)
        plans = pltpu.with_memory_space_constraint(deal_plan.transpose(1, 2, 3, 0), pltpu.HBM)
        any_ = pl.BlockSpec(memory_space=pl.ANY)
        hbm = pl.BlockSpec(memory_space=pltpu.HBM)
        vmem = pl.BlockSpec(memory_space=pltpu.VMEM)
        dma = pltpu.SemaphoreType.DMA
        results = pl.pallas_call(
            functools.partial(kernel, n_dp, n_ctx, n_lane, sub),
            out_shape=(
                pltpu.VMEM((tok, width), bf),
                pltpu.VMEM((tok, width), bf),
                pltpu.VMEM((tok, HEAD), bf),
                pltpu.VMEM((tok, HEAD), bf),
            ),
            in_specs=[hbm] * 6,
            out_specs=(any_, any_, vmem, vmem),
            scratch_shapes=[
                pltpu.VMEM((n_dp, sub, n_lane * width), bf),
                pltpu.VMEM((n_dp, sub, n_lane * HEAD), bf),
                pltpu.VMEM((n_dp, sub, n_lane * HEAD), bf),
                pltpu.VMEM((n_dp, sub, n_lane * width), bf),
                pltpu.SMEM(doc_lengths.shape, jnp.int32),
                pltpu.SMEM((n_lane, n_dp, n_ctx), jnp.int32),
                pltpu.VMEM((peers, sub, width), bf),
                pltpu.VMEM((peers, sub, 2 * HEAD), bf),
                pltpu.VMEM((peers, sub, width), bf),
                pltpu.VMEM((tok, width), bf),
                pltpu.VMEM((NEARBY * tok, 2 * HEAD), bf),
                pltpu.VMEM((tok, width), bf),
                pltpu.VMEM((NEARBY * tok, tok), f32),
                pltpu.VMEM((QUERY_GROUP, NEARBY * tok, tok), f32),
                pltpu.VMEM((HEAD, NEARBY * tok), bf),
                pltpu.VMEM((HEAD, NEARBY * tok), bf),
                pltpu.VMEM((QUERY_GROUP, HEAD, tok), bf),
                pltpu.VMEM((QUERY_GROUP, 1, tok), f32),
                pltpu.VMEM((QUERY_GROUP, HEAD, tok), f32),
                pltpu.VMEM((NEARBY - 1, tok, 2 * HEAD), bf),
                pltpu.VMEM((NEARBY - 1, tok, 2 * HEAD), bf),
                pltpu.VMEM((NEARBY * tok, 2 * HEAD), f32),
                pltpu.VMEM((tok, width), bf),
                pltpu.VMEM((tok, width), bf),
                dma((4,)),
                dma((2,)),
                dma((len(Q_GROUPS), 2)),
                dma((2,)),
                dma((len(G_GROUPS), 2)),
                dma((NEARBY - 1,)),
                dma((NEARBY - 1,)),
                dma((NEARBY - 1,)),
                dma((NEARBY - 1,)),
                dma((2,)),
            ],
            compiler_params=pltpu.CompilerParams(
                collective_id=0, has_side_effects=True, vmem_limit_bytes=48 * 1024 * 1024
            ),
        )(*split, lengths, plans)
        return pl.pallas_call(
            store,
            out_shape=tuple(pltpu.HBM(a.shape, a.dtype) for a in results),
            in_specs=[vmem] * 4,
            out_specs=(hbm,) * 4,
            scratch_shapes=[dma((4,))],
        )(*[pltpu.with_memory_space_constraint(a, pltpu.VMEM) for a in results])

    arriving = P(("dp", "context", "tensor"), None)
    leaving = P(("dp", "context"), "tensor")
    return jax.shard_map(
        on_device,
        mesh=mesh,
        in_specs=(arriving, arriving, arriving, arriving, P(), P()),
        out_specs=(leaving, leaving, leaving, leaving),
        check_vma=False,
    )
```

```python
import functools

import jax
import jax.numpy as jnp
from jax import lax
from jax.experimental import pallas as pl
from jax.experimental.pallas import tpu as pltpu
from jax.sharding import PartitionSpec as P

HEAD = 128
QUERY_GROUP = 8
NEARBY = 3
MESH = pl.DeviceIdType.MESH
Q_GROUPS = ((0, 4), (4, 8))
G_GROUPS = ((0, 4), (4, 6), (6, 7), (7, 8))
MASKED = -1e30
SCALE = HEAD ** (-0.5)
LOG2E = 1.4426950408889634

NT = (((1,), (1,)), ((), ()))
NN = (((1,), (0,)), ((), ()))


def dot(a, b, dims):
    return lax.dot_general(a, b, dims, preferred_element_type=jnp.float32)


def kernel(
    n_dp, n_ctx, n_lane, sub,
    q_hbm, k_hbm, v_hbm, g_hbm, lengths_hbm, plan_hbm,
    out_hbm, dq_hbm, dk_ref, dv_ref,
    q_in, k_in, v_in, g_in, lengths, plan,
    q_send, kv_send, g_send, q_rows, kv_rows, g_rows,
    bias, probs, kt, vt, gt, delta, dqt, part_send, part_recv, dkv_acc, out_buf, dq_buf,
    in_sem, plan_sem, q_sems, kv_sems, g_sems, halo_send, halo_recv, back_send, back_recv, out_sem,
):
    s = lax.axis_index("dp")
    c = lax.axis_index("context")
    t = lax.axis_index("tensor")
    peers = n_dp * n_lane
    me = s * n_lane + t
    tok = peers * sub
    width = QUERY_GROUP * HEAD

    def ctx(by):
        return {"context": lax.rem(c + by + n_ctx, n_ctx)}

    def peer(i):
        r = lax.rem(s + i // n_lane, n_dp)
        lane = lax.rem(t + lax.rem(i, n_lane), n_lane)
        return r, lane

    barrier = pltpu.get_barrier_semaphore()

    def greet(i, carry):
        r, lane = peer(i)
        pl.semaphore_signal(
            barrier, inc=1, device_id={"dp": r, "tensor": lane}, device_id_type=MESH
        )
        return carry

    lax.fori_loop(1, peers, greet, 0)
    for by in (-2, -1, 1, 2):
        pl.semaphore_signal(barrier, inc=1, device_id=ctx(by), device_id_type=MESH)

    plan_copy = pltpu.make_async_copy(plan_hbm.at[s], plan, plan_sem.at[0])
    plan_copy.start()
    lengths_copy = pltpu.make_async_copy(lengths_hbm, lengths, plan_sem.at[1])
    lengths_copy.start()
    loads = [
        pltpu.make_async_copy(a, b, in_sem.at[n])
        for n, (a, b) in enumerate(
            ((k_hbm, k_in), (v_hbm, v_in), (q_hbm, q_in), (g_hbm, g_in))
        )
    ]
    for copy in loads:
        copy.start()
    plan_copy.wait()
    lengths_copy.wait()
    for copy in loads:
        copy.wait()

    for r in range(n_dp):
        block = jnp.int32(0)
        for b in range(n_dp):
            block = jnp.where(plan[t, b, c] == r, jnp.int32(b), block)
        k_block = k_in[block]
        v_block = v_in[block]
        for lane in range(n_lane):
            kv_send[r * n_lane + lane, :, 0:HEAD] = k_block[:, lane * HEAD : (lane + 1) * HEAD]
            kv_send[r * n_lane + lane, :, HEAD:] = v_block[:, lane * HEAD : (lane + 1) * HEAD]
        q_block = q_in[block]
        g_block = g_in[block]
        for lane in range(n_lane):
            q_send[r * n_lane + lane] = q_block[:, lane * width : (lane + 1) * width]
            g_send[r * n_lane + lane] = g_block[:, lane * width : (lane + 1) * width]

    p = c * tok + lax.broadcasted_iota(jnp.int32, (1, tok), 1)

    def next_bound(n, carry):
        bound, start = carry
        bound = bound + lengths[s, n]
        return bound, jnp.maximum(start, jnp.where(bound <= p, bound, 0))

    _, start = lax.fori_loop(
        0, lengths.shape[1], next_bound, (jnp.int32(0), jnp.zeros((1, tok), jnp.int32))
    )
    j = (c - (NEARBY - 1)) * tok + lax.broadcasted_iota(jnp.int32, (NEARBY * tok, 1), 0)
    bias[...] = jnp.where((j <= p) & (j >= start), 0.0, MASKED).astype(jnp.float32)

    pl.semaphore_wait(barrier, peers - 1 + 4)

    own = (NEARBY - 1) * tok

    def my_rows(base):
        return pl.ds(pl.multiple_of(base + me * sub, sub), sub)

    def deal(sent, rows, base, sems, cols):
        def one(i, carry):
            r, lane = peer(i)
            pltpu.make_async_remote_copy(
                src_ref=sent.at[r * n_lane + lane, :, cols],
                dst_ref=rows.at[my_rows(base), cols],
                send_sem=sems.at[0],
                recv_sem=sems.at[1],
                device_id={"dp": r, "tensor": lane},
                device_id_type=MESH,
            ).start()
            return carry

        lax.fori_loop(1, peers, one, 0)
        pltpu.make_async_copy(
            sent.at[me, :, cols], rows.at[my_rows(base), cols], sems.at[1]
        ).start()

    def columns(group):
        return pl.ds(group[0] * HEAD, (group[1] - group[0]) * HEAD)

    def arrived(rows, sems):
        pltpu.make_async_copy(rows, rows, sems.at[1]).wait()

    deals = [
        (kv_send, kv_rows, own, kv_sems, pl.ds(0, 2 * HEAD)),
    ]
    for n, group in enumerate(Q_GROUPS):
        deals.append((q_send, q_rows, 0, q_sems.at[n], columns(group)))
    for n, group in enumerate(G_GROUPS):
        deals.append((g_send, g_rows, 0, g_sems.at[n], columns(group)))
    for one_deal in deals:
        deal(*one_deal)

    own_kv = kv_rows.at[pl.ds(own, tok)]
    arrived(own_kv, kv_sems)
    halo = []
    for d in range(1, NEARBY):
        copy = pltpu.make_async_remote_copy(
            src_ref=own_kv,
            dst_ref=kv_rows.at[pl.ds(own - d * tok, tok)],
            send_sem=halo_send.at[d - 1],
            recv_sem=halo_recv.at[d - 1],
            device_id=ctx(d),
            device_id_type=MESH,
        )
        copy.start()
        halo.append(copy)
    for copy in halo:
        copy.wait()
    kt[...] = kv_rows[:, 0:HEAD].astype(jnp.float32).T.astype(jnp.bfloat16)
    vt[...] = kv_rows[:, HEAD:].astype(jnp.float32).T.astype(jnp.bfloat16)

    def head(h):
        return pl.ds(pl.multiple_of(h * HEAD, HEAD), HEAD)

    def forward(h, carry):
        scores = dot(kv_rows[:, 0:HEAD], q_rows[:, head(h)], NT) * (SCALE * LOG2E) + bias[...]
        top = jnp.max(scores, axis=0, keepdims=True)
        e = jnp.exp2(scores - top)
        pr = e * (1.0 / jnp.sum(e, axis=0, keepdims=True))
        probs[h] = pr
        o = dot(vt[...], pr.astype(jnp.bfloat16), NN)
        out_buf[:, head(h)] = o.T.astype(jnp.bfloat16)
        return carry

    dkv_acc[...] = jnp.zeros_like(dkv_acc)
    for n, group in enumerate(Q_GROUPS):
        arrived(q_rows.at[:, columns(group)], q_sems.at[n])
        lax.fori_loop(*group, forward, 0)
    out_copy = pltpu.make_async_copy(out_buf, out_hbm, out_sem.at[0])
    out_copy.start()

    def turn(h):
        g_f = g_rows[:, head(h)].astype(jnp.float32).T
        o_t = out_buf[:, head(h)].astype(jnp.float32).T
        gt[h] = g_f.astype(jnp.bfloat16)
        delta[h] = jnp.sum(g_f * o_t, axis=0, keepdims=True)

    def backward(n, h):
        at = pl.ds(n * tok, tok)
        pr = probs[h, at]
        dprob = dot(kv_rows[at, HEAD:], gt[h], NN)
        ds = (SCALE * pr * (dprob - delta[h])).astype(jnp.bfloat16)
        term = dot(kt[:, at], ds, NN)
        total = term if n == 0 else dqt[h] + term
        if n == NEARBY - 1:
            dq_buf[:, head(h)] = total.T.astype(jnp.bfloat16)
        else:
            dqt[h] = total
        dkv_acc[at, 0:HEAD] += dot(ds, q_rows[:, head(h)], NN)
        dkv_acc[at, HEAD:] += dot(pr.astype(jnp.bfloat16), g_rows[:, head(h)], NN)

    back = []

    def send_part(n):
        copy = pltpu.make_async_remote_copy(
            src_ref=part_send.at[n],
            dst_ref=part_recv.at[n],
            send_sem=back_send.at[n],
            recv_sem=back_recv.at[n],
            device_id=ctx(n - (NEARBY - 1)),
            device_id_type=MESH,
        )
        copy.start()
        back.append(copy)

    for n, group in enumerate(G_GROUPS[:-1]):
        arrived(g_rows.at[:, columns(group)], g_sems.at[n])

        def whole(h, carry):
            turn(h)
            for m in range(NEARBY):
                backward(m, h)
            return carry

        lax.fori_loop(*group, whole, 0)

    first, end = G_GROUPS[-1]
    arrived(g_rows.at[:, columns(G_GROUPS[-1])], g_sems.at[len(G_GROUPS) - 1])
    for h in range(first, end):
        turn(h)
    for m in range(NEARBY):
        for h in range(first, end):
            backward(m, h)
            if h == first and m > 0:
                send_part(m - 1)
        if m < NEARBY - 1:
            part_send[m] = dkv_acc[m * tok : (m + 1) * tok].astype(jnp.bfloat16)

    dq_copy = pltpu.make_async_copy(dq_buf, dq_hbm, out_sem.at[1])
    dq_copy.start()
    for copy in back:
        copy.wait()
    total = dkv_acc[own:]
    for n in range(NEARBY - 1):
        total = total + part_recv[n].astype(jnp.float32)
    dk_ref[...] = total[:, 0:HEAD].astype(jnp.bfloat16)
    dv_ref[...] = total[:, HEAD:].astype(jnp.bfloat16)

    for sent, _, _, sems, cols in deals:
        gone = sent.at[pl.ds(0, peers - 1), :, cols]
        pltpu.make_async_copy(gone, gone, sems.at[0]).wait()
    out_copy.wait()
    dq_copy.wait()


def store(*refs):
    sems = refs[8]
    copies = [pltpu.make_async_copy(refs[n], refs[n + 4], sems.at[n]) for n in range(4)]
    for copy in copies:
        copy.start()
    for copy in copies:
        copy.wait()


def solution(mesh):
    n_dp, n_ctx, n_lane = (mesh.shape[a] for a in ("dp", "context", "tensor"))

    def on_device(queries, keys, values, grad_out, doc_lengths, deal_plan):
        rows = queries.shape[0]
        sub = rows // n_dp
        peers = n_dp * n_lane
        tok = peers * sub
        width = QUERY_GROUP * HEAD
        bf, f32 = jnp.bfloat16, jnp.float32
        split = [
            pltpu.with_memory_space_constraint(a.reshape(n_dp, sub, a.shape[1]), pltpu.HBM)
            for a in (queries, keys, values, grad_out)
        ]
        lengths = pltpu.with_memory_space_constraint(doc_lengths, pltpu.HBM)
        plans = pltpu.with_memory_space_constraint(deal_plan.transpose(1, 2, 3, 0), pltpu.HBM)
        any_ = pl.BlockSpec(memory_space=pl.ANY)
        hbm = pl.BlockSpec(memory_space=pltpu.HBM)
        vmem = pl.BlockSpec(memory_space=pltpu.VMEM)
        dma = pltpu.SemaphoreType.DMA
        results = pl.pallas_call(
            functools.partial(kernel, n_dp, n_ctx, n_lane, sub),
            out_shape=(
                pltpu.VMEM((tok, width), bf),
                pltpu.VMEM((tok, width), bf),
                pltpu.VMEM((tok, HEAD), bf),
                pltpu.VMEM((tok, HEAD), bf),
            ),
            in_specs=[hbm] * 6,
            out_specs=(any_, any_, vmem, vmem),
            scratch_shapes=[
                pltpu.VMEM((n_dp, sub, n_lane * width), bf),
                pltpu.VMEM((n_dp, sub, n_lane * HEAD), bf),
                pltpu.VMEM((n_dp, sub, n_lane * HEAD), bf),
                pltpu.VMEM((n_dp, sub, n_lane * width), bf),
                pltpu.SMEM(doc_lengths.shape, jnp.int32),
                pltpu.SMEM((n_lane, n_dp, n_ctx), jnp.int32),
                pltpu.VMEM((peers, sub, width), bf),
                pltpu.VMEM((peers, sub, 2 * HEAD), bf),
                pltpu.VMEM((peers, sub, width), bf),
                pltpu.VMEM((tok, width), bf),
                pltpu.VMEM((NEARBY * tok, 2 * HEAD), bf),
                pltpu.VMEM((tok, width), bf),
                pltpu.VMEM((NEARBY * tok, tok), f32),
                pltpu.VMEM((QUERY_GROUP, NEARBY * tok, tok), f32),
                pltpu.VMEM((HEAD, NEARBY * tok), bf),
                pltpu.VMEM((HEAD, NEARBY * tok), bf),
                pltpu.VMEM((QUERY_GROUP, HEAD, tok), bf),
                pltpu.VMEM((QUERY_GROUP, 1, tok), f32),
                pltpu.VMEM((QUERY_GROUP, HEAD, tok), f32),
                pltpu.VMEM((NEARBY - 1, tok, 2 * HEAD), bf),
                pltpu.VMEM((NEARBY - 1, tok, 2 * HEAD), bf),
                pltpu.VMEM((NEARBY * tok, 2 * HEAD), f32),
                pltpu.VMEM((tok, width), bf),
                pltpu.VMEM((tok, width), bf),
                dma((4,)),
                dma((2,)),
                dma((len(Q_GROUPS), 2)),
                dma((2,)),
                dma((len(G_GROUPS), 2)),
                dma((NEARBY - 1,)),
                dma((NEARBY - 1,)),
                dma((NEARBY - 1,)),
                dma((NEARBY - 1,)),
                dma((2,)),
            ],
            compiler_params=pltpu.CompilerParams(
                collective_id=0, has_side_effects=True, vmem_limit_bytes=48 * 1024 * 1024
            ),
        )(*split, lengths, plans)
        return pl.pallas_call(
            store,
            out_shape=tuple(pltpu.HBM(a.shape, a.dtype) for a in results),
            in_specs=[vmem] * 4,
            out_specs=(hbm,) * 4,
            scratch_shapes=[dma((4,))],
        )(*[pltpu.with_memory_space_constraint(a, pltpu.VMEM) for a in results])

    arriving = P(("dp", "context", "tensor"), None)
    leaving = P(("dp", "context"), "tensor")
    return jax.shard_map(
        on_device,
        mesh=mesh,
        in_specs=(arriving, arriving, arriving, arriving, P(), P()),
        out_specs=(leaving, leaving, leaving, leaving),
        check_vma=False,
    )
```

```python
import functools

import jax
import jax.numpy as jnp
from jax import lax
from jax.experimental import pallas as pl
from jax.experimental.pallas import tpu as pltpu
from jax.sharding import PartitionSpec as P

HEAD = 128
QUERY_GROUP = 8
NEARBY = 3
MESH = pl.DeviceIdType.MESH
Q_GROUPS = ((0, 4), (4, 8))
G_GROUPS = ((0, 4), (4, 7), (7, 8))
MASKED = -1e30
SCALE = HEAD ** (-0.5)
LOG2E = 1.4426950408889634

NT = (((1,), (1,)), ((), ()))
NN = (((1,), (0,)), ((), ()))


def dot(a, b, dims):
    return lax.dot_general(a, b, dims, preferred_element_type=jnp.float32)


def kernel(
    n_dp, n_ctx, n_lane, sub,
    q_hbm, k_hbm, v_hbm, g_hbm, lengths_hbm, plan_hbm,
    out_hbm, dq_hbm, dk_ref, dv_ref,
    q_in, k_in, v_in, g_in, lengths, plan,
    q_send, kv_send, g_send, q_rows, kv_rows, g_rows,
    bias, probs, kt, vt, gt, delta, dqt, part_send, part_recv, dkv_acc, out_buf, dq_buf,
    in_sem, plan_sem, q_sems, kv_sems, g_sems, halo_send, halo_recv, back_send, back_recv, out_sem,
):
    s = lax.axis_index("dp")
    c = lax.axis_index("context")
    t = lax.axis_index("tensor")
    peers = n_dp * n_lane
    me = s * n_lane + t
    tok = peers * sub
    width = QUERY_GROUP * HEAD

    def ctx(by):
        return {"context": lax.rem(c + by + n_ctx, n_ctx)}

    def peer(i):
        r = lax.rem(s + i // n_lane, n_dp)
        lane = lax.rem(t + lax.rem(i, n_lane), n_lane)
        return r, lane

    barrier = pltpu.get_barrier_semaphore()

    def greet(i, carry):
        r, lane = peer(i)
        pl.semaphore_signal(
            barrier, inc=1, device_id={"dp": r, "tensor": lane}, device_id_type=MESH
        )
        return carry

    lax.fori_loop(1, peers, greet, 0)
    for by in (-2, -1, 1, 2):
        pl.semaphore_signal(barrier, inc=1, device_id=ctx(by), device_id_type=MESH)

    plan_copy = pltpu.make_async_copy(plan_hbm.at[s], plan, plan_sem.at[0])
    plan_copy.start()
    lengths_copy = pltpu.make_async_copy(lengths_hbm, lengths, plan_sem.at[1])
    lengths_copy.start()
    loads = [
        pltpu.make_async_copy(a, b, in_sem.at[n])
        for n, (a, b) in enumerate(
            ((k_hbm, k_in), (v_hbm, v_in), (q_hbm, q_in), (g_hbm, g_in))
        )
    ]
    for copy in loads:
        copy.start()
    plan_copy.wait()
    lengths_copy.wait()
    for copy in loads:
        copy.wait()

    for r in range(n_dp):
        block = jnp.int32(0)
        for b in range(n_dp):
            block = jnp.where(plan[t, b, c] == r, jnp.int32(b), block)
        k_block = k_in[block]
        v_block = v_in[block]
        for lane in range(n_lane):
            kv_send[r * n_lane + lane, :, 0:HEAD] = k_block[:, lane * HEAD : (lane + 1) * HEAD]
            kv_send[r * n_lane + lane, :, HEAD:] = v_block[:, lane * HEAD : (lane + 1) * HEAD]
        q_block = q_in[block]
        g_block = g_in[block]
        for lane in range(n_lane):
            q_send[r * n_lane + lane] = q_block[:, lane * width : (lane + 1) * width]
            g_send[r * n_lane + lane] = g_block[:, lane * width : (lane + 1) * width]

    p = c * tok + lax.broadcasted_iota(jnp.int32, (1, tok), 1)

    def next_bound(n, carry):
        bound, start = carry
        bound = bound + lengths[s, n]
        return bound, jnp.maximum(start, jnp.where(bound <= p, bound, 0))

    _, start = lax.fori_loop(
        0, lengths.shape[1], next_bound, (jnp.int32(0), jnp.zeros((1, tok), jnp.int32))
    )
    j = (c - (NEARBY - 1)) * tok + lax.broadcasted_iota(jnp.int32, (NEARBY * tok, 1), 0)
    bias[...] = jnp.where((j <= p) & (j >= start), 0.0, MASKED).astype(jnp.float32)

    pl.semaphore_wait(barrier, peers - 1 + 4)

    own = (NEARBY - 1) * tok

    def my_rows(base):
        return pl.ds(pl.multiple_of(base + me * sub, sub), sub)

    def deal(sent, rows, base, sems, cols):
        def one(i, carry):
            r, lane = peer(i)
            pltpu.make_async_remote_copy(
                src_ref=sent.at[r * n_lane + lane, :, cols],
                dst_ref=rows.at[my_rows(base), cols],
                send_sem=sems.at[0],
                recv_sem=sems.at[1],
                device_id={"dp": r, "tensor": lane},
                device_id_type=MESH,
            ).start()
            return carry

        lax.fori_loop(1, peers, one, 0)
        pltpu.make_async_copy(
            sent.at[me, :, cols], rows.at[my_rows(base), cols], sems.at[1]
        ).start()

    def columns(group):
        return pl.ds(group[0] * HEAD, (group[1] - group[0]) * HEAD)

    def arrived(rows, sems):
        pltpu.make_async_copy(rows, rows, sems.at[1]).wait()

    deals = [
        (kv_send, kv_rows, own, kv_sems, pl.ds(0, 2 * HEAD)),
    ]
    for n, group in enumerate(Q_GROUPS):
        deals.append((q_send, q_rows, 0, q_sems.at[n], columns(group)))
    for n, group in enumerate(G_GROUPS):
        deals.append((g_send, g_rows, 0, g_sems.at[n], columns(group)))
    for one_deal in deals[:2]:
        deal(*one_deal)

    own_kv = kv_rows.at[pl.ds(own, tok)]
    arrived(own_kv, kv_sems)
    halo = []
    for d in range(1, NEARBY):
        copy = pltpu.make_async_remote_copy(
            src_ref=own_kv,
            dst_ref=kv_rows.at[pl.ds(own - d * tok, tok)],
            send_sem=halo_send.at[d - 1],
            recv_sem=halo_recv.at[d - 1],
            device_id=ctx(d),
            device_id_type=MESH,
        )
        copy.start()
        halo.append(copy)
    for one_deal in deals[2:]:
        deal(*one_deal)
    for copy in halo:
        copy.wait()
    kt[...] = kv_rows[:, 0:HEAD].astype(jnp.float32).T.astype(jnp.bfloat16)
    vt[...] = kv_rows[:, HEAD:].astype(jnp.float32).T.astype(jnp.bfloat16)

    def head(h):
        return pl.ds(pl.multiple_of(h * HEAD, HEAD), HEAD)

    def forward(h, carry):
        scores = dot(kv_rows[:, 0:HEAD], q_rows[:, head(h)], NT) * (SCALE * LOG2E) + bias[...]
        top = jnp.max(scores, axis=0, keepdims=True)
        e = jnp.exp2(scores - top)
        pr = e * (1.0 / jnp.sum(e, axis=0, keepdims=True))
        probs[h] = pr
        o = dot(vt[...], pr.astype(jnp.bfloat16), NN)
        out_buf[:, head(h)] = o.T.astype(jnp.bfloat16)
        return carry

    dkv_acc[...] = jnp.zeros_like(dkv_acc)
    for n, group in enumerate(Q_GROUPS):
        arrived(q_rows.at[:, columns(group)], q_sems.at[n])
        lax.fori_loop(*group, forward, 0)
    out_copy = pltpu.make_async_copy(out_buf, out_hbm, out_sem.at[0])
    out_copy.start()

    def turn(h):
        g_f = g_rows[:, head(h)].astype(jnp.float32).T
        o_t = out_buf[:, head(h)].astype(jnp.float32).T
        gt[h] = g_f.astype(jnp.bfloat16)
        delta[h] = jnp.sum(g_f * o_t, axis=0, keepdims=True)

    def backward(n, h):
        at = pl.ds(n * tok, tok)
        pr = probs[h, at]
        dprob = dot(kv_rows[at, HEAD:], gt[h], NN)
        ds = (SCALE * pr * (dprob - delta[h])).astype(jnp.bfloat16)
        term = dot(kt[:, at], ds, NN)
        total = term if n == 0 else dqt[h] + term
        if n == NEARBY - 1:
            dq_buf[:, head(h)] = total.T.astype(jnp.bfloat16)
        else:
            dqt[h] = total
        dkv_acc[at, 0:HEAD] += dot(ds, q_rows[:, head(h)], NN)
        dkv_acc[at, HEAD:] += dot(pr.astype(jnp.bfloat16), g_rows[:, head(h)], NN)

    back = []

    def send_part(n):
        copy = pltpu.make_async_remote_copy(
            src_ref=part_send.at[n],
            dst_ref=part_recv.at[n],
            send_sem=back_send.at[n],
            recv_sem=back_recv.at[n],
            device_id=ctx(n - (NEARBY - 1)),
            device_id_type=MESH,
        )
        copy.start()
        back.append(copy)

    for n, group in enumerate(G_GROUPS[:-1]):
        arrived(g_rows.at[:, columns(group)], g_sems.at[n])

        def whole(h, carry):
            turn(h)
            for m in range(NEARBY):
                backward(m, h)
            return carry

        lax.fori_loop(*group, whole, 0)

    first, end = G_GROUPS[-1]
    arrived(g_rows.at[:, columns(G_GROUPS[-1])], g_sems.at[len(G_GROUPS) - 1])
    for h in range(first, end):
        turn(h)
    for m in range(NEARBY):
        for h in range(first, end):
            backward(m, h)
            if h == first and m > 0:
                send_part(m - 1)
        if m < NEARBY - 1:
            part_send[m] = dkv_acc[m * tok : (m + 1) * tok].astype(jnp.bfloat16)

    dq_copy = pltpu.make_async_copy(dq_buf, dq_hbm, out_sem.at[1])
    dq_copy.start()
    for copy in back:
        copy.wait()
    total = dkv_acc[own:]
    for n in range(NEARBY - 1):
        total = total + part_recv[n].astype(jnp.float32)
    dk_ref[...] = total[:, 0:HEAD].astype(jnp.bfloat16)
    dv_ref[...] = total[:, HEAD:].astype(jnp.bfloat16)

    for sent, _, _, sems, cols in deals:
        gone = sent.at[pl.ds(0, peers - 1), :, cols]
        pltpu.make_async_copy(gone, gone, sems.at[0]).wait()
    out_copy.wait()
    dq_copy.wait()


def store(*refs):
    sems = refs[8]
    copies = [pltpu.make_async_copy(refs[n], refs[n + 4], sems.at[n]) for n in range(4)]
    for copy in copies:
        copy.start()
    for copy in copies:
        copy.wait()


def solution(mesh):
    n_dp, n_ctx, n_lane = (mesh.shape[a] for a in ("dp", "context", "tensor"))

    def on_device(queries, keys, values, grad_out, doc_lengths, deal_plan):
        rows = queries.shape[0]
        sub = rows // n_dp
        peers = n_dp * n_lane
        tok = peers * sub
        width = QUERY_GROUP * HEAD
        bf, f32 = jnp.bfloat16, jnp.float32
        split = [
            pltpu.with_memory_space_constraint(a.reshape(n_dp, sub, a.shape[1]), pltpu.HBM)
            for a in (queries, keys, values, grad_out)
        ]
        lengths = pltpu.with_memory_space_constraint(doc_lengths, pltpu.HBM)
        plans = pltpu.with_memory_space_constraint(deal_plan.transpose(1, 2, 3, 0), pltpu.HBM)
        any_ = pl.BlockSpec(memory_space=pl.ANY)
        hbm = pl.BlockSpec(memory_space=pltpu.HBM)
        vmem = pl.BlockSpec(memory_space=pltpu.VMEM)
        dma = pltpu.SemaphoreType.DMA
        results = pl.pallas_call(
            functools.partial(kernel, n_dp, n_ctx, n_lane, sub),
            out_shape=(
                pltpu.VMEM((tok, width), bf),
                pltpu.VMEM((tok, width), bf),
                pltpu.VMEM((tok, HEAD), bf),
                pltpu.VMEM((tok, HEAD), bf),
            ),
            in_specs=[hbm] * 6,
            out_specs=(any_, any_, vmem, vmem),
            scratch_shapes=[
                pltpu.VMEM((n_dp, sub, n_lane * width), bf),
                pltpu.VMEM((n_dp, sub, n_lane * HEAD), bf),
                pltpu.VMEM((n_dp, sub, n_lane * HEAD), bf),
                pltpu.VMEM((n_dp, sub, n_lane * width), bf),
                pltpu.SMEM(doc_lengths.shape, jnp.int32),
                pltpu.SMEM((n_lane, n_dp, n_ctx), jnp.int32),
                pltpu.VMEM((peers, sub, width), bf),
                pltpu.VMEM((peers, sub, 2 * HEAD), bf),
                pltpu.VMEM((peers, sub, width), bf),
                pltpu.VMEM((tok, width), bf),
                pltpu.VMEM((NEARBY * tok, 2 * HEAD), bf),
                pltpu.VMEM((tok, width), bf),
                pltpu.VMEM((NEARBY * tok, tok), f32),
                pltpu.VMEM((QUERY_GROUP, NEARBY * tok, tok), f32),
                pltpu.VMEM((HEAD, NEARBY * tok), bf),
                pltpu.VMEM((HEAD, NEARBY * tok), bf),
                pltpu.VMEM((QUERY_GROUP, HEAD, tok), bf),
                pltpu.VMEM((QUERY_GROUP, 1, tok), f32),
                pltpu.VMEM((QUERY_GROUP, HEAD, tok), f32),
                pltpu.VMEM((NEARBY - 1, tok, 2 * HEAD), bf),
                pltpu.VMEM((NEARBY - 1, tok, 2 * HEAD), bf),
                pltpu.VMEM((NEARBY * tok, 2 * HEAD), f32),
                pltpu.VMEM((tok, width), bf),
                pltpu.VMEM((tok, width), bf),
                dma((4,)),
                dma((2,)),
                dma((len(Q_GROUPS), 2)),
                dma((2,)),
                dma((len(G_GROUPS), 2)),
                dma((NEARBY - 1,)),
                dma((NEARBY - 1,)),
                dma((NEARBY - 1,)),
                dma((NEARBY - 1,)),
                dma((2,)),
            ],
            compiler_params=pltpu.CompilerParams(
                collective_id=0, has_side_effects=True, vmem_limit_bytes=48 * 1024 * 1024
            ),
        )(*split, lengths, plans)
        return pl.pallas_call(
            store,
            out_shape=tuple(pltpu.HBM(a.shape, a.dtype) for a in results),
            in_specs=[vmem] * 4,
            out_specs=(hbm,) * 4,
            scratch_shapes=[dma((4,))],
        )(*[pltpu.with_memory_space_constraint(a, pltpu.VMEM) for a in results])

    arriving = P(("dp", "context", "tensor"), None)
    leaving = P(("dp", "context"), "tensor")
    return jax.shard_map(
        on_device,
        mesh=mesh,
        in_specs=(arriving, arriving, arriving, arriving, P(), P()),
        out_specs=(leaving, leaving, leaving, leaving),
        check_vma=False,
    )
```
